512 devices in a mesh: row: 32 (over z, y_hi), col: 16 (over y_lo, x, core).
Axes of the slice: x: 4, y: 8 (y_hi: 4, y_lo: 2; y = y_hi * 2 + y_lo), z: 8, core: 2. Of those that a mesh axis runs over, the one named last changes fastest.
Arguments:
- inverse_block: bfloat16 [20480, 20480], P('row', 'col')
- factor_cols: bfloat16 [3, 20480, 512], P(None, 'col', 'row'), may hold values from -6 to 6
- occupancy: int32 [3, 160], replicated, may hold values 0 or 1
- row_block: int32 [3, 160], replicated, may hold values from 0 to 159, each once within a row
- coupling: bfloat16 [2, 512, 512], replicated, may hold values from -0.25 to 0.25
- diag_inverse: float32 [3, 512, 512], P(None, None, 'col'), may hold values from -6 to 6
Outputs:
- columns: float32 [3, 20480, 512], P(None, ('row', 'col'))
- diagonals: float32 [3, 512, 512], P(None, None, 'col')
The draws below stay inside these ranges and needn't reach their ends.
Inputs may be any that keep to these rules, and one draw needn't show every extreme that they name: `row_block`: each row names every one of the 160 row blocks exactly once.
All inputs are finite; a program needn't handle non-finite values.
Results may differ from the reference program's by a relative error of at most 0.0003.
Values may be sent and summed in bfloat16 or wider, within the bound.
A program may use at most 64 MiB of HBM per device.

```python
import jax
import jax.numpy as jnp
from jax import lax

W = 512
SUPER = 3
ROWS = 20480
NB = 160


def draw_inverse_block(key, part):
    first_key, second_key = jax.random.split(jax.random.fold_in(key, 7))
    spread = jax.random.normal(first_key, (ROWS, ROWS), jnp.float32)
    leading = jax.random.uniform(second_key, (ROWS,), jnp.float32, 1.0, 3.0)
    spread = spread * ROWS ** (-0.5)
    steps = jnp.arange(ROWS, dtype=jnp.int32)
    return spread.at[steps, steps].add(leading).astype(jnp.bfloat16)


def plant(entries, stream_key, least, high):
    extent = entries.shape
    index_at = [jax.random.randint(jax.random.fold_in(stream_key, axis), (), 0, extent[axis]) for axis in range(len(extent))]
    entries = entries.at[tuple(index_at)].set(least)
    longest = extent.index(max(extent))
    index_at[longest] = (index_at[longest] + 1) % extent[longest]
    return entries.at[tuple(index_at)].set(high)


def steps_of(own_key, extent, cuts, low, high):
    level, own = 1.0, jax.random.fold_in(own_key, 6)
    for dim, blocks in cuts:
        steps = jnp.exp(jax.random.uniform(jax.random.fold_in(own, dim), (blocks,), jnp.float32, low / len(cuts), high / len(cuts)))
        level = level * jnp.repeat(steps, extent[dim] // blocks).reshape([-1 if axis == dim else 1 for axis in range(len(extent))])
    return level


def normal_values(own_key, shape, scale, most, shards=(), kind=jnp.bfloat16):
    factor_of = steps_of(own_key, shape, shards, -0.22, 0.18) if shards else 1.0
    array = jax.random.normal(own_key, shape, jnp.float32) * scale * factor_of
    return jnp.minimum(jnp.maximum(array, -most), most).astype(kind)


def setup_inputs(seed: int = 0) -> dict:
    streams_of = jax.random.split(jax.random.key(seed), 7)
    inverse_block = draw_inverse_block(jax.random.fold_in(streams_of[6], 71), 0)
    factor_cols = normal_values(streams_of[1], (SUPER, ROWS, W), 1.0, 6.0, ((1, 16), (2, 32)))
    occupancy = plant((jax.random.randint(streams_of[2], (SUPER, NB), 0, 20) < 17).astype(jnp.int32), jax.random.fold_in(streams_of[2], 1), 0, 1)
    row_block = jax.vmap(lambda own: jax.random.permutation(own, NB))(jax.random.split(streams_of[3], SUPER)).reshape((SUPER, NB)).astype(jnp.int32)
    coupling = normal_values(streams_of[4], (SUPER - 1, W, W), W ** -0.5, 0.25)
    diag_inverse = normal_values(streams_of[5], (SUPER, W, W), 1.0, 6.0, ((2, 16),), jnp.float32)
    return {"inverse_block": inverse_block, "factor_cols": factor_cols, "occupancy": occupancy, "row_block": row_block, "coupling": coupling, "diag_inverse": diag_inverse}


def reference(inverse_block, factor_cols, occupancy, row_block, coupling, diag_inverse):
    highest = lax.Precision.HIGHEST
    nblocks = ROWS // 128
    previous = None
    chain_prev = None
    column_list = []
    diag_list = []
    for position in range(SUPER):
        blocks = factor_cols[position].reshape(nblocks, 128, W) * occupancy[position][:, None, None].astype(jnp.bfloat16)
        placed = jnp.zeros_like(blocks).at[row_block[position]].set(blocks).reshape(ROWS, W)
        product = jnp.dot(inverse_block, placed, preferred_element_type=jnp.float32)
        if position == 0:
            coupled = jnp.zeros((ROWS, W), jnp.float32)
        else:
            coupled = jnp.dot(previous, coupling[position - 1].astype(jnp.float32), precision=highest)
        current = -(product + coupled)
        own = placed.astype(jnp.float32)
        inner = jnp.dot(own.T, current, precision=highest) - jnp.dot(coupled.T, own, precision=highest)
        diag_now = diag_inverse[position] - inner / ROWS
        if position > 0:
            link = coupling[position - 1].astype(jnp.float32)
            diag_now = diag_now + jnp.dot(link.T, jnp.dot(chain_prev, link, precision=highest), precision=highest)
        column_list.append(current)
        diag_list.append(diag_now)
        previous = current
        chain_prev = diag_now
    return jnp.stack(column_list), jnp.stack(diag_list)
```

```python
import jax
import jax.numpy as jnp
from jax import lax
from jax.experimental import pallas as pl
from jax.experimental.pallas import tpu as pltpu
from jax.sharding import PartitionSpec as P

highest = lax.Precision.HIGHEST
MESH = pl.DeviceIdType.MESH
ZS, YH = 8, 4
CHIPS = 8


def greet(peers):
    barrier = pltpu.get_barrier_semaphore()
    for peer in peers:
        pl.semaphore_signal(barrier, inc=1, device_id=peer, device_id_type=MESH)
    pl.semaphore_wait(barrier, len(peers))


def push(src, dst, send_sem, recv_sem, device):
    return pltpu.make_async_remote_copy(
        src_ref=src,
        dst_ref=dst,
        send_sem=send_sem,
        recv_sem=recv_sem,
        device_id=device,
        device_id_type=MESH,
    )


def gather_col_kernel(x_ref, out_ref, local_sem, send_sem, pass_sem, recv_sem):
    row, col = lax.axis_index("row"), lax.axis_index("col")
    chip, core = col // 2, lax.rem(col, 2)
    partner = (row, chip * 2 + 1 - core)
    chips = [lax.rem(chip + j, CHIPS) for j in range(1, CHIPS)]
    greet([(row, other * 2 + core) for other in chips] + [partner])
    mine = pltpu.make_async_copy(x_ref, out_ref.at[col], local_sem)
    mine.start()
    copies = []
    for j, other in enumerate(chips):
        copies.append(push(x_ref, out_ref.at[col], send_sem.at[j], recv_sem.at[col], (row, other * 2 + core)))
    copies.append(push(x_ref, out_ref.at[col], pass_sem.at[0], recv_sem.at[col], partner))
    for copy in copies:
        copy.start()
    for j in range(1, CHIPS):
        other = lax.rem(chip + CHIPS - j, CHIPS)
        slot = other * 2 + core
        landed = push(x_ref, out_ref.at[slot], pass_sem.at[j], recv_sem.at[slot], partner)
        landed.wait_recv()
        onward = push(out_ref.at[slot], out_ref.at[slot], pass_sem.at[j], recv_sem.at[slot], partner)
        onward.start()
        copies.append(onward)
    for j in range(CHIPS):
        slot = lax.rem(chip + j, CHIPS) * 2 + 1 - core
        push(x_ref, out_ref.at[slot], pass_sem.at[0], recv_sem.at[slot], partner).wait_recv()
    for copy in copies:
        copy.wait_send()
    mine.wait()


def gather_col(x):
    return pl.pallas_call(
        gather_col_kernel,
        out_shape=jax.ShapeDtypeStruct((CHIPS * 2,) + x.shape, x.dtype),
        in_specs=[pl.BlockSpec(memory_space=pl.ANY)],
        out_specs=pl.BlockSpec(memory_space=pl.ANY),
        scratch_shapes=[
            pltpu.SemaphoreType.DMA,
            pltpu.SemaphoreType.DMA((CHIPS - 1,)),
            pltpu.SemaphoreType.DMA((CHIPS,)),
            pltpu.SemaphoreType.DMA((CHIPS * 2,)),
        ],
        compiler_params=pltpu.CompilerParams(collective_id=0, has_side_effects=True),
        name="gather_col",
    )(x)


def gather_row_kernel(x_ref, out_ref, local_sem, y_sem, z_sem, recv_sem):
    row, col = lax.axis_index("row"), lax.axis_index("col")
    z, y = row // YH, lax.rem(row, YH)
    right = (lax.rem(z + 1, ZS) * YH + y, col)
    left = (lax.rem(z + ZS - 1, ZS) * YH + y, col)
    others = [(z * YH + lax.rem(y + j, YH), col) for j in range(1, YH)]
    greet(others + [right, left])
    mine = pltpu.make_async_copy(x_ref, out_ref.at[:, row], local_sem)
    mine.start()
    copies = []

    def send(src, slot, sem, device):
        copy = push(src, out_ref.at[:, slot], sem, recv_sem.at[slot], device)
        copy.start()
        copies.append(copy)

    def arrive(slot):
        push(x_ref, out_ref.at[:, slot], local_sem, recv_sem.at[slot], right).wait_recv()

    send(x_ref, row, z_sem.at[0, 0, 0], right)
    send(x_ref, row, z_sem.at[1, 0, 0], left)
    for j in range(1, YH):
        send(x_ref, row, y_sem.at[j - 1], others[j - 1])
    for j in range(1, YH):
        slot = z * YH + lax.rem(y + j, YH)
        arrive(slot)
        send(out_ref.at[:, slot], slot, z_sem.at[0, j, 0], right)
        send(out_ref.at[:, slot], slot, z_sem.at[1, j, 0], left)
    for hop in range(1, ZS // 2 + 1):
        for j in range(YH):
            lane = lax.rem(y + j, YH)
            far_right = ZS // 2 - j % 2
            for way, far, at, device in (
                (0, far_right, lax.rem(z + ZS - hop, ZS), right),
                (1, ZS - 1 - far_right, lax.rem(z + hop, ZS), left),
            ):
                slot = at * YH + lane
                if hop <= far:
                    arrive(slot)
                if hop < far:
                    send(out_ref.at[:, slot], slot, z_sem.at[way, j, hop], device)
    for copy in copies:
        copy.wait_send()
    mine.wait()


def gather_row(x):
    supers, width_part, span = x.shape
    return pl.pallas_call(
        gather_row_kernel,
        out_shape=jax.ShapeDtypeStruct((supers, ZS * YH, width_part, span), x.dtype),
        in_specs=[pl.BlockSpec(memory_space=pl.ANY)],
        out_specs=pl.BlockSpec(memory_space=pl.ANY),
        scratch_shapes=[
            pltpu.SemaphoreType.DMA,
            pltpu.SemaphoreType.DMA((YH - 1,)),
            pltpu.SemaphoreType.DMA((2, YH, ZS // 2)),
            pltpu.SemaphoreType.DMA((ZS * YH,)),
        ],
        compiler_params=pltpu.CompilerParams(collective_id=1, has_side_effects=True),
        name="gather_row",
    )(x)


def swap_core_kernel(x_ref, out_ref, send_sem, recv_sem):
    row, col = lax.axis_index("row"), lax.axis_index("col")
    chip, core = col // 2, lax.rem(col, 2)
    partner = (row, chip * 2 + 1 - core)
    greet([partner])
    copy = push(x_ref.at[:, 1 - core], out_ref, send_sem, recv_sem, partner)
    copy.start()
    copy.wait()


def swap_core(x, ident):
    return pl.pallas_call(
        swap_core_kernel,
        out_shape=jax.ShapeDtypeStruct(x.shape[:1] + x.shape[2:], x.dtype),
        in_specs=[pl.BlockSpec(memory_space=pl.ANY)],
        out_specs=pl.BlockSpec(memory_space=pl.ANY),
        scratch_shapes=[pltpu.SemaphoreType.DMA, pltpu.SemaphoreType.DMA],
        compiler_params=pltpu.CompilerParams(collective_id=ident, has_side_effects=True),
        name="swap_core_%d" % ident,
    )(x)


def swap_chips_kernel(x_ref, out_ref, local_sem, send_sem, recv_sem):
    row, col = lax.axis_index("row"), lax.axis_index("col")
    chip, core = col // 2, lax.rem(col, 2)
    chips = [lax.rem(chip + j, CHIPS) for j in range(1, CHIPS)]
    greet([(row, other * 2 + core) for other in chips])
    mine = pltpu.make_async_copy(x_ref.at[chip], out_ref.at[chip], local_sem)
    mine.start()
    copies = [
        push(x_ref.at[other], out_ref.at[chip], send_sem.at[j], recv_sem.at[chip], (row, other * 2 + core))
        for j, other in enumerate(chips)
    ]
    for copy in copies:
        copy.start()
    for j, other in enumerate(chips):
        push(x_ref.at[other], out_ref.at[other], send_sem.at[j], recv_sem.at[other], (row, other * 2 + core)).wait_recv()
    for copy in copies:
        copy.wait_send()
    mine.wait()


def swap_chips(x, ident):
    return pl.pallas_call(
        swap_chips_kernel,
        out_shape=jax.ShapeDtypeStruct(x.shape, x.dtype),
        in_specs=[pl.BlockSpec(memory_space=pl.ANY)],
        out_specs=pl.BlockSpec(memory_space=pl.ANY),
        scratch_shapes=[
            pltpu.SemaphoreType.DMA,
            pltpu.SemaphoreType.DMA((CHIPS - 1,)),
            pltpu.SemaphoreType.DMA((CHIPS,)),
        ],
        compiler_params=pltpu.CompilerParams(collective_id=ident, has_side_effects=True),
        name="swap_chips_%d" % ident,
    )(x)


def scatter_sum(x, core, ident):
    grid = x.reshape((CHIPS, 2) + x.shape[1:])
    other = swap_core(grid, ident)
    own = lax.dynamic_index_in_dim(grid, core, 1, keepdims=False)
    return jnp.sum(swap_chips(own + other, ident + 1), axis=0)


def place_kernel(row_block_ref, occupancy_ref, column_ref, blocks_ref, placed_ref, part_ref):
    supers, nblocks = placed_ref.shape[:2]
    per = blocks_ref.shape[2]
    for s in range(supers):

        def step(device, carry, s=s):
            for k in range(per):
                b = device * per + k
                block = blocks_ref[device, s, k]
                keep = occupancy_ref[s, b] > 0
                placed_ref[s, row_block_ref[s, b]] = jnp.where(keep, block, jnp.zeros_like(block))
            return carry

        lax.fori_loop(0, nblocks // per, step, 0)
    first = column_ref[0] * per
    for s in range(supers):
        for k in range(per):
            part_ref[s, :, k * 128 : (k + 1) * 128] = placed_ref[s, first + k]


def place(blocks, occupancy, row_block, column):
    devices, supers, per, width_part, tall = blocks.shape
    smem = pl.BlockSpec(memory_space=pltpu.SMEM)
    vmem = pl.BlockSpec(memory_space=pltpu.VMEM)
    return pl.pallas_call(
        place_kernel,
        out_shape=(
            jax.ShapeDtypeStruct((supers, devices * per, width_part, tall), blocks.dtype),
            jax.ShapeDtypeStruct((supers, width_part, per * tall), blocks.dtype),
        ),
        in_specs=[smem, smem, smem, vmem],
        out_specs=(vmem, vmem),
        name="place",
    )(row_block, occupancy, column.reshape(1).astype(jnp.int32), blocks)


def dot_high(a, b):
    return jnp.dot(a, b, precision=highest)


def per_device(inverse_block, factor_cols, occupancy, row_block, coupling, diag_inverse):
    column = lax.axis_index("col")
    core = lax.rem(column, 2)
    row_first = (lax.axis_index("row") == 0).astype(jnp.float32)
    row_parts = lax.axis_size("row")
    col_parts = lax.axis_size("col")
    local_rows = inverse_block.shape[0]
    rows_total = local_rows * row_parts
    supers, span, width_part = factor_cols.shape
    width = width_part * row_parts
    tile = local_rows // col_parts
    diag_cols = diag_inverse.shape[2]
    per = span // 128

    packed = jnp.transpose(factor_cols.reshape(supers, per, 128, width_part), (0, 1, 3, 2))
    placed, part = place(gather_col(packed), occupancy, row_block, column)

    per_row = local_rows // 128
    block_at = jnp.minimum(column * tile // 128, per_row - 2)
    near = lax.dynamic_slice_in_dim(
        placed.reshape(supers, row_parts, per_row, width_part, 128), block_at, 2, 2
    )
    near = jnp.transpose(near, (0, 1, 3, 2, 4)).reshape(supers, row_parts, width_part, 256)
    outgoing = lax.dynamic_slice_in_dim(near, column * tile - block_at * 128, tile, 3)
    arrived = lax.all_to_all(outgoing, "row", split_axis=1, concat_axis=1, tiled=True)
    own_rows = arrived.reshape(supers, width, tile).astype(jnp.float32)

    panel = gather_row(part).reshape(supers * width, span)
    term = lax.dot_general(
        inverse_block, panel, (((1,), (1,)), ((), ())), preferred_element_type=jnp.float32
    )
    summed = scatter_sum(term.reshape(col_parts, tile, supers * width), core, 2)

    columns = []
    chain = []
    for s in range(supers):
        product = summed[:, s * width : (s + 1) * width]
        own = own_rows[s]
        if s == 0:
            current = -product
            inner = dot_high(current.T, own.T)
        else:
            link = coupling[s - 1].astype(jnp.float32)
            coupled = dot_high(columns[-1], link)
            current = -(product + coupled)
            inner = dot_high(current.T, own.T) - dot_high(own, coupled)
        embedded = lax.dynamic_update_slice(
            jnp.zeros((width, width), jnp.float32), diag_inverse[s].T, (column * diag_cols, 0)
        )
        total = row_first * embedded - inner / rows_total
        if s > 0:
            total = total + dot_high(link.T, dot_high(chain[-1], link))
        columns.append(current)
        chain.append(total)
    partial = jnp.stack([t.reshape(col_parts, diag_cols, width) for t in chain], axis=1)
    mine = scatter_sum(partial.reshape(col_parts, supers * diag_cols, width), core, 4)
    diagonals = jnp.transpose(lax.psum(mine, "row").reshape(supers, diag_cols, width), (0, 2, 1))
    return (jnp.stack(columns), diagonals)


def solution(mesh):
    in_specs = (P("row", "col"), P(None, "col", "row"), P(), P(), P(), P(None, None, "col"))
    out_specs = (P(None, ("row", "col"), None), P(None, None, "col"))
    return jax.shard_map(
        per_device, mesh=mesh, in_specs=in_specs, out_specs=out_specs, check_vma=False
    )
```

```python
import jax
import jax.numpy as jnp
from jax import lax
from jax.experimental import pallas as pl
from jax.experimental.pallas import tpu as pltpu
from jax.sharding import PartitionSpec as P

highest = lax.Precision.HIGHEST
MESH = pl.DeviceIdType.MESH
ZS, YH = 8, 4
CHIPS, XS = 8, 4


def greet(peers):
    barrier = pltpu.get_barrier_semaphore()
    for peer in peers:
        pl.semaphore_signal(barrier, inc=1, device_id=peer, device_id_type=MESH)
    pl.semaphore_wait(barrier, len(peers))


def push(src, dst, send_sem, recv_sem, device):
    return pltpu.make_async_remote_copy(
        src_ref=src,
        dst_ref=dst,
        send_sem=send_sem,
        recv_sem=recv_sem,
        device_id=device,
        device_id_type=MESH,
    )


def ring_position():
    row, col = lax.axis_index("row"), lax.axis_index("col")
    chip, core = col // 2, lax.rem(col, 2)
    x, y = lax.rem(chip, XS), chip // XS

    def at(dx, dy):
        return (y if dy == 0 else 1 - y) * XS + lax.rem(x + dx, XS)

    return row, core, at


NEAR = ((1, 0), (XS - 1, 0), (0, 1), (1, 1), (XS - 1, 1))


def gather_col_kernel(x_ref, out_ref, local_sem, send_sem, pass_sem, turn_sem, half_sem, recv_sem):
    row, core, at = ring_position()
    chip = at(0, 0)
    col = chip * 2 + core
    partner = (row, chip * 2 + 1 - core)
    half = x_ref.shape[0] // 2
    parts = (pl.ds(0, half), pl.ds(half, x_ref.shape[0] - half))
    greet([(row, at(*step) * 2 + core) for step in NEAR] + [partner])
    mine = pltpu.make_async_copy(x_ref, out_ref.at[col], local_sem)
    mine.start()
    copies = []

    def send(src, dst, sem, landing, device):
        copy = push(src, dst, sem, landing, device)
        copy.start()
        copies.append(copy)

    for j, step in enumerate(NEAR):
        send(x_ref, out_ref.at[col], send_sem.at[j], recv_sem.at[col], (row, at(*step) * 2 + core))
    send(x_ref, out_ref.at[col], pass_sem.at[0], recv_sem.at[col], partner)
    for j, step in enumerate(NEAR):
        slot = at(*step) * 2 + core
        push(x_ref, out_ref.at[slot], local_sem, recv_sem.at[slot], partner).wait_recv()
        if step[1] == 0:
            piece = out_ref.at[slot, parts[j]]
            for dy in range(2):
                device = (row, at(XS - step[0], dy) * 2 + core)
                send(piece, piece, turn_sem.at[j, dy], half_sem.at[j, dy], device)
        send(out_ref.at[slot], out_ref.at[slot], pass_sem.at[1 + j], recv_sem.at[slot], partner)
    for dy in range(2):
        slot = at(2, dy) * 2 + core
        for j in range(2):
            piece = out_ref.at[slot, parts[j]]
            push(piece, piece, local_sem, half_sem.at[j, dy], partner).wait_recv()
        send(out_ref.at[slot], out_ref.at[slot], pass_sem.at[6 + dy], recv_sem.at[slot], partner)
    for step in ((0, 0),) + NEAR + ((2, 0), (2, 1)):
        slot = at(*step) * 2 + 1 - core
        push(x_ref, out_ref.at[slot], local_sem, recv_sem.at[slot], partner).wait_recv()
    for copy in copies:
        copy.wait_send()
    mine.wait()


def gather_col(x):
    return pl.pallas_call(
        gather_col_kernel,
        out_shape=jax.ShapeDtypeStruct((CHIPS * 2,) + x.shape, x.dtype),
        in_specs=[pl.BlockSpec(memory_space=pl.ANY)],
        out_specs=pl.BlockSpec(memory_space=pl.ANY),
        scratch_shapes=[
            pltpu.SemaphoreType.DMA,
            pltpu.SemaphoreType.DMA((len(NEAR),)),
            pltpu.SemaphoreType.DMA((CHIPS,)),
            pltpu.SemaphoreType.DMA((2, 2)),
            pltpu.SemaphoreType.DMA((2, 2)),
            pltpu.SemaphoreType.DMA((CHIPS * 2,)),
        ],
        compiler_params=pltpu.CompilerParams(collective_id=0, has_side_effects=True),
        name="gather_col",
    )(x)


def gather_row_kernel(x_ref, out_ref, local_sem, y_sem, z_sem, recv_sem):
    row, col = lax.axis_index("row"), lax.axis_index("col")
    z, y = row // YH, lax.rem(row, YH)
    right = (lax.rem(z + 1, ZS) * YH + y, col)
    left = (lax.rem(z + ZS - 1, ZS) * YH + y, col)
    others = [(z * YH + lax.rem(y + j, YH), col) for j in range(1, YH)]
    greet(others + [right, left])
    mine = pltpu.make_async_copy(x_ref, out_ref.at[:, row], local_sem)
    mine.start()
    copies = []

    def send(src, slot, sem, device):
        copy = push(src, out_ref.at[:, slot], sem, recv_sem.at[slot], device)
        copy.start()
        copies.append(copy)

    def arrive(slot):
        push(x_ref, out_ref.at[:, slot], local_sem, recv_sem.at[slot], right).wait_recv()

    send(x_ref, row, z_sem.at[0, 0, 0], right)
    send(x_ref, row, z_sem.at[1, 0, 0], left)
    for j in range(1, YH):
        send(x_ref, row, y_sem.at[j - 1], others[j - 1])
    for j in range(1, YH):
        slot = z * YH + lax.rem(y + j, YH)
        arrive(slot)
        send(out_ref.at[:, slot], slot, z_sem.at[0, j, 0], right)
        send(out_ref.at[:, slot], slot, z_sem.at[1, j, 0], left)
    for hop in range(1, ZS // 2 + 1):
        for j in range(YH):
            lane = lax.rem(y + j, YH)
            far_right = ZS // 2 - j % 2
            for way, far, at, device in (
                (0, far_right, lax.rem(z + ZS - hop, ZS), right),
                (1, ZS - 1 - far_right, lax.rem(z + hop, ZS), left),
            ):
                slot = at * YH + lane
                if hop <= far:
                    arrive(slot)
                if hop < far:
                    send(out_ref.at[:, slot], slot, z_sem.at[way, j, hop], device)
    for copy in copies:
        copy.wait_send()
    mine.wait()


def gather_row(x, ident):
    supers, width_part, span = x.shape
    return pl.pallas_call(
        gather_row_kernel,
        out_shape=jax.ShapeDtypeStruct((supers, ZS * YH, width_part, span), x.dtype),
        in_specs=[pl.BlockSpec(memory_space=pl.ANY)],
        out_specs=pl.BlockSpec(memory_space=pl.ANY),
        scratch_shapes=[
            pltpu.SemaphoreType.DMA,
            pltpu.SemaphoreType.DMA((YH - 1,)),
            pltpu.SemaphoreType.DMA((2, YH, ZS // 2)),
            pltpu.SemaphoreType.DMA((ZS * YH,)),
        ],
        compiler_params=pltpu.CompilerParams(collective_id=ident, has_side_effects=True),
        name="gather_row_%d" % ident,
    )(x)


def swap_core_kernel(x_ref, out_ref, send_sem, recv_sem):
    row, col = lax.axis_index("row"), lax.axis_index("col")
    chip, core = col // 2, lax.rem(col, 2)
    partner = (row, chip * 2 + 1 - core)
    greet([partner])
    copy = push(x_ref.at[:, 1 - core], out_ref, send_sem, recv_sem, partner)
    copy.start()
    copy.wait()


def swap_core(x, ident):
    return pl.pallas_call(
        swap_core_kernel,
        out_shape=jax.ShapeDtypeStruct(x.shape[:1] + x.shape[2:], x.dtype),
        in_specs=[pl.BlockSpec(memory_space=pl.ANY)],
        out_specs=pl.BlockSpec(memory_space=pl.ANY),
        scratch_shapes=[pltpu.SemaphoreType.DMA, pltpu.SemaphoreType.DMA],
        compiler_params=pltpu.CompilerParams(collective_id=ident, has_side_effects=True),
        name="swap_core_%d" % ident,
    )(x)


def swap_chips_kernel(x_ref, out_ref, relay, local_sem, send_sem, away_sem, turn_sem, relay_sem, half_sem, recv_sem):
    row, core, at = ring_position()
    chip = at(0, 0)
    rows = x_ref.shape[1]
    cut = rows // 16 * 8
    parts = (pl.ds(0, cut), pl.ds(cut, rows - cut))
    sizes = (cut, rows - cut)

    def device(step):
        return (row, at(*step) * 2 + core)

    greet([device(step) for step in NEAR])
    mine = pltpu.make_async_copy(x_ref.at[chip], out_ref.at[chip], local_sem)
    mine.start()
    copies = []

    def send(src, dst, sem, landing, device):
        copy = push(src, dst, sem, landing, device)
        copy.start()
        copies.append(copy)

    def held(j, dy):
        return relay.at[j, dy, pl.ds(0, sizes[j])]

    for dy in range(2):
        for j in range(2):
            send(x_ref.at[at(2, dy), parts[j]], held(j, dy), away_sem.at[j, dy], relay_sem.at[j, dy], device(NEAR[j]))
    for j, step in enumerate(NEAR):
        send(x_ref.at[at(*step)], out_ref.at[chip], send_sem.at[j], recv_sem.at[chip], device(step))
    for dy in range(2):
        for j in range(2):
            origin = at(XS - NEAR[j][0], 0)
            push(held(j, dy), held(j, dy), local_sem, relay_sem.at[j, dy], device(NEAR[j])).wait_recv()
            target = device((NEAR[j][0], dy))
            send(held(j, dy), out_ref.at[origin, parts[j]], turn_sem.at[j, dy], half_sem.at[j, dy], target)
    for step in NEAR:
        other = at(*step)
        push(x_ref.at[other], out_ref.at[other], local_sem, recv_sem.at[other], device(step)).wait_recv()
    for dy in range(2):
        for j in range(2):
            piece = out_ref.at[at(2, dy), parts[j]]
            push(piece, piece, local_sem, half_sem.at[j, dy], device(NEAR[0])).wait_recv()
    for copy in copies:
        copy.wait_send()
    mine.wait()


def swap_chips(x, ident):
    chips, rows, lanes = x.shape
    four = pltpu.SemaphoreType.DMA((2, 2))
    return pl.pallas_call(
        swap_chips_kernel,
        out_shape=jax.ShapeDtypeStruct(x.shape, x.dtype),
        in_specs=[pl.BlockSpec(memory_space=pl.ANY)],
        out_specs=pl.BlockSpec(memory_space=pl.ANY),
        scratch_shapes=[
            pltpu.VMEM((2, 2, rows - rows // 16 * 8, lanes), x.dtype),
            pltpu.SemaphoreType.DMA,
            pltpu.SemaphoreType.DMA((len(NEAR),)),
            four,
            four,
            four,
            four,
            pltpu.SemaphoreType.DMA((chips,)),
        ],
        compiler_params=pltpu.CompilerParams(collective_id=ident, has_side_effects=True),
        name="swap_chips_%d" % ident,
    )(x)


def swap_row_kernel(along_z, x_ref, out_ref, local_sem, send_sem, recv_sem):
    row, col = lax.axis_index("row"), lax.axis_index("col")
    z, y = row // YH, lax.rem(row, YH)
    count = x_ref.shape[0]
    me = z if along_z else y
    others = [lax.rem(me + j, count) for j in range(1, count)]
    devices = [(other * YH + y if along_z else z * YH + other, col) for other in others]
    greet(devices)
    mine = pltpu.make_async_copy(x_ref.at[me], out_ref.at[me], local_sem)
    mine.start()
    copies = [
        push(x_ref.at[other], out_ref.at[me], send_sem.at[j], recv_sem.at[me], devices[j])
        for j, other in enumerate(others)
    ]
    for copy in copies:
        copy.start()
    for j, other in enumerate(others):
        push(x_ref.at[other], out_ref.at[other], send_sem.at[j], recv_sem.at[other], devices[j]).wait_recv()
    for copy in copies:
        copy.wait_send()
    mine.wait()


def swap_row(x, along_z, ident):
    count = x.shape[0]

    def kernel(*refs):
        swap_row_kernel(along_z, *refs)

    return pl.pallas_call(
        kernel,
        out_shape=jax.ShapeDtypeStruct(x.shape, x.dtype),
        in_specs=[pl.BlockSpec(memory_space=pl.ANY)],
        out_specs=pl.BlockSpec(memory_space=pl.ANY),
        scratch_shapes=[
            pltpu.SemaphoreType.DMA,
            pltpu.SemaphoreType.DMA((count - 1,)),
            pltpu.SemaphoreType.DMA((count,)),
        ],
        compiler_params=pltpu.CompilerParams(collective_id=ident, has_side_effects=True),
        name="swap_row_%d" % ident,
    )(x)


def sum_row(x, ident):
    rows, lanes = x.shape
    piece = jnp.sum(swap_row(x.reshape(YH, rows // YH, lanes), False, ident), axis=0)
    piece = piece.reshape(ZS, rows // (YH * ZS), lanes)
    piece = jnp.sum(swap_row(piece, True, ident + 1), axis=0)
    whole = gather_row(piece[None], ident + 2).reshape(ZS, YH, -1, lanes)
    return jnp.transpose(whole, (1, 0, 2, 3)).reshape(rows, lanes)


def scatter_sum(x, core, ident):
    grid = x.reshape((CHIPS, 2) + x.shape[1:])
    other = swap_core(grid, ident)
    own = lax.dynamic_index_in_dim(grid, core, 1, keepdims=False)
    return jnp.sum(swap_chips(own + other, ident + 1), axis=0)


def place_kernel(row_block_ref, occupancy_ref, column_ref, blocks_ref, placed_ref, part_ref):
    supers, nblocks = placed_ref.shape[:2]
    per = blocks_ref.shape[2]
    for s in range(supers):

        def step(device, carry, s=s):
            for k in range(per):
                b = device * per + k
                block = blocks_ref[device, s, k]
                keep = occupancy_ref[s, b] > 0
                placed_ref[s, row_block_ref[s, b]] = jnp.where(keep, block, jnp.zeros_like(block))
            return carry

        lax.fori_loop(0, nblocks // per, step, 0)
    first = column_ref[0] * per
    for s in range(supers):
        for k in range(per):
            part_ref[s, :, k * 128 : (k + 1) * 128] = placed_ref[s, first + k]


def place(blocks, occupancy, row_block, column):
    devices, supers, per, width_part, tall = blocks.shape
    smem = pl.BlockSpec(memory_space=pltpu.SMEM)
    vmem = pl.BlockSpec(memory_space=pltpu.VMEM)
    return pl.pallas_call(
        place_kernel,
        out_shape=(
            jax.ShapeDtypeStruct((supers, devices * per, width_part, tall), blocks.dtype),
            jax.ShapeDtypeStruct((supers, width_part, per * tall), blocks.dtype),
        ),
        in_specs=[smem, smem, smem, vmem],
        out_specs=(vmem, vmem),
        name="place",
    )(row_block, occupancy, column.reshape(1).astype(jnp.int32), blocks)


def dot_high(a, b):
    return jnp.dot(a, b, precision=highest)


def per_device(inverse_block, factor_cols, occupancy, row_block, coupling, diag_inverse):
    column = lax.axis_index("col")
    core = lax.rem(column, 2)
    row_first = (lax.axis_index("row") == 0).astype(jnp.float32)
    row_parts = lax.axis_size("row")
    col_parts = lax.axis_size("col")
    local_rows = inverse_block.shape[0]
    rows_total = local_rows * row_parts
    supers, span, width_part = factor_cols.shape
    width = width_part * row_parts
    tile = local_rows // col_parts
    diag_cols = diag_inverse.shape[2]
    per = span // 128

    packed = jnp.transpose(factor_cols.reshape(supers, per, 128, width_part), (0, 1, 3, 2))
    placed, part = place(gather_col(packed), occupancy, row_block, column)

    per_row = local_rows // 128
    block_at = jnp.minimum(column * tile // 128, per_row - 2)
    near = lax.dynamic_slice_in_dim(
        placed.reshape(supers, row_parts, per_row, width_part, 128), block_at, 2, 2
    )
    near = jnp.transpose(near, (0, 1, 3, 2, 4)).reshape(supers, row_parts, width_part, 256)
    outgoing = lax.dynamic_slice_in_dim(near, column * tile - block_at * 128, tile, 3)
    arrived = lax.all_to_all(outgoing, "row", split_axis=1, concat_axis=1, tiled=True)
    own_rows = arrived.reshape(supers, width, tile).astype(jnp.float32)

    panel = gather_row(part, 1).reshape(supers * width, span)
    term = lax.dot_general(
        inverse_block, panel, (((1,), (1,)), ((), ())), preferred_element_type=jnp.float32
    )
    summed = scatter_sum(term.reshape(col_parts, tile, supers * width), core, 2)

    columns = []
    chain = []
    for s in range(supers):
        product = summed[:, s * width : (s + 1) * width]
        own = own_rows[s]
        if s == 0:
            current = -product
            inner = dot_high(current.T, own.T)
        else:
            link = coupling[s - 1].astype(jnp.float32)
            coupled = dot_high(columns[-1], link)
            current = -(product + coupled)
            inner = dot_high(current.T, own.T) - dot_high(own, coupled)
        embedded = lax.dynamic_update_slice(
            jnp.zeros((width, width), jnp.float32), diag_inverse[s].T, (column * diag_cols, 0)
        )
        total = row_first * embedded - inner / rows_total
        if s > 0:
            total = total + dot_high(link.T, dot_high(chain[-1], link))
        columns.append(current)
        chain.append(total)
    partial = jnp.stack([t.reshape(col_parts, diag_cols, width) for t in chain], axis=1)
    mine = scatter_sum(partial.reshape(col_parts, supers * diag_cols, width), core, 4)
    diagonals = jnp.transpose(sum_row(mine, 6).reshape(supers, diag_cols, width), (0, 2, 1))
    return (jnp.stack(columns), diagonals)


def solution(mesh):
    in_specs = (P("row", "col"), P(None, "col", "row"), P(), P(), P(), P(None, None, "col"))
    out_specs = (P(None, ("row", "col"), None), P(None, None, "col"))
    return jax.shard_map(
        per_device, mesh=mesh, in_specs=in_specs, out_specs=out_specs, check_vma=False
    )
```

```python
import jax
import jax.numpy as jnp
from jax import lax
from jax.experimental import pallas as pl
from jax.experimental.pallas import tpu as pltpu
from jax.sharding import PartitionSpec as P

highest = lax.Precision.HIGHEST
MESH = pl.DeviceIdType.MESH
ZS, YH = 8, 4
CHIPS, XS = 8, 4


def greet(peers):
    barrier = pltpu.get_barrier_semaphore()
    for peer in peers:
        pl.semaphore_signal(barrier, inc=1, device_id=peer, device_id_type=MESH)
    pl.semaphore_wait(barrier, len(peers))


def push(src, dst, send_sem, recv_sem, device):
    return pltpu.make_async_remote_copy(
        src_ref=src,
        dst_ref=dst,
        send_sem=send_sem,
        recv_sem=recv_sem,
        device_id=device,
        device_id_type=MESH,
    )


def ring_position():
    row, col = lax.axis_index("row"), lax.axis_index("col")
    chip, core = col // 2, lax.rem(col, 2)
    x, y = lax.rem(chip, XS), chip // XS

    def at(dx, dy):
        return (y if dy == 0 else 1 - y) * XS + lax.rem(x + dx, XS)

    return row, core, at


NEAR = ((1, 0), (XS - 1, 0), (0, 1), (1, 1), (XS - 1, 1))


def gather_col_kernel(x_ref, out_ref, local_sem, send_sem, pass_sem, turn_sem, half_sem, recv_sem):
    row, core, at = ring_position()
    chip = at(0, 0)
    col = chip * 2 + core
    partner = (row, chip * 2 + 1 - core)
    half = x_ref.shape[0] // 2
    parts = (pl.ds(0, half), pl.ds(half, x_ref.shape[0] - half))
    greet([(row, at(*step) * 2 + core) for step in NEAR] + [partner])
    mine = pltpu.make_async_copy(x_ref, out_ref.at[col], local_sem)
    mine.start()
    copies = []

    def send(src, dst, sem, landing, device):
        copy = push(src, dst, sem, landing, device)
        copy.start()
        copies.append(copy)

    for j, step in enumerate(NEAR):
        send(x_ref, out_ref.at[col], send_sem.at[j], recv_sem.at[col], (row, at(*step) * 2 + core))
    send(x_ref, out_ref.at[col], pass_sem.at[0], recv_sem.at[col], partner)
    for j, step in enumerate(NEAR):
        slot = at(*step) * 2 + core
        push(x_ref, out_ref.at[slot], local_sem, recv_sem.at[slot], partner).wait_recv()
        if step[1] == 0:
            piece = out_ref.at[slot, parts[j]]
            for dy in range(2):
                device = (row, at(XS - step[0], dy) * 2 + core)
                send(piece, piece, turn_sem.at[j, dy], half_sem.at[j, dy], device)
        send(out_ref.at[slot], out_ref.at[slot], pass_sem.at[1 + j], recv_sem.at[slot], partner)
    for dy in range(2):
        slot = at(2, dy) * 2 + core
        for j in range(2):
            piece = out_ref.at[slot, parts[j]]
            push(piece, piece, local_sem, half_sem.at[j, dy], partner).wait_recv()
        send(out_ref.at[slot], out_ref.at[slot], pass_sem.at[6 + dy], recv_sem.at[slot], partner)
    for step in ((0, 0),) + NEAR + ((2, 0), (2, 1)):
        slot = at(*step) * 2 + 1 - core
        push(x_ref, out_ref.at[slot], local_sem, recv_sem.at[slot], partner).wait_recv()
    for copy in copies:
        copy.wait_send()
    mine.wait()


def gather_col(x):
    return pl.pallas_call(
        gather_col_kernel,
        out_shape=jax.ShapeDtypeStruct((CHIPS * 2,) + x.shape, x.dtype),
        in_specs=[pl.BlockSpec(memory_space=pl.ANY)],
        out_specs=pl.BlockSpec(memory_space=pl.ANY),
        scratch_shapes=[
            pltpu.SemaphoreType.DMA,
            pltpu.SemaphoreType.DMA((len(NEAR),)),
            pltpu.SemaphoreType.DMA((CHIPS,)),
            pltpu.SemaphoreType.DMA((2, 2)),
            pltpu.SemaphoreType.DMA((2, 2)),
            pltpu.SemaphoreType.DMA((CHIPS * 2,)),
        ],
        compiler_params=pltpu.CompilerParams(collective_id=0, has_side_effects=True),
        name="gather_col",
    )(x)


def gather_row_kernel(x_ref, rows_ref, out_ref, own_ref, staged, local_sem, send_sem, wide_sem, thin_sem, z_sem, y_sem):
    row, col = lax.axis_index("row"), lax.axis_index("col")
    z, y = row // YH, lax.rem(row, YH)
    last = x_ref.shape[0] - 1
    parts = (pl.ds(0, last), pl.ds(last, 1))
    sems = (wide_sem, thin_sem)

    def at(dz, dy):
        return lax.rem(z + dz + ZS, ZS) * YH + lax.rem(y + dy + YH, YH)

    def device(dz, dy):
        return (at(dz, dy), col)

    zs, ys = range(1, ZS), range(1, YH)
    greet([device(dz, 0) for dz in zs] + [device(0, dy) for dy in ys])
    locals_ = [pltpu.make_async_copy(x_ref, out_ref.at[:, row], local_sem.at[0])]
    locals_.append(pltpu.make_async_copy(rows_ref.at[z], staged.at[z], local_sem.at[1]))
    for copy in locals_:
        copy.start()
    copies = []

    def send(src, dst, landing, where):
        copy = push(src, dst, send_sem.at[len(copies)], landing, where)
        copy.start()
        copies.append(copy)

    def block(kind, slot):
        return out_ref.at[parts[kind], slot]

    def onward(kind, slot, where, first=False):
        src = x_ref.at[parts[kind]] if first else block(kind, slot)
        send(src, block(kind, slot), sems[kind].at[slot], where)

    def arrive(kind, slot):
        piece = block(kind, slot)
        push(piece, piece, local_sem.at[0], sems[kind].at[slot], device(1, 0)).wait_recv()

    right, left, up, down = device(1, 0), device(-1, 0), device(0, 1), device(0, -1)
    for where in (right, left):
        onward(1, row, where, True)
    for where in (up, down):
        onward(0, row, where, True)
    for where in (right, left):
        onward(0, row, where, True)
    for where in (up, down):
        onward(1, row, where, True)
    for dz in zs:
        there = lax.rem(z + dz, ZS)
        send(rows_ref.at[there], staged.at[z], z_sem.at[z], device(dz, 0))

    for dy in (-1, 1, 2):
        slot = at(0, dy)
        arrive(0, slot)
        if dy == -1:
            onward(0, slot, up)
        onward(0, slot, right)
        onward(0, slot, left)

    half = ZS // 2

    def cross(dz):
        arrive(1, at(dz, -1))
        if dz % 2 == 0:
            onward(1, at(dz, -1), up)
        arrive(1, at(dz, 1))
        if dz % 2 == 1:
            onward(1, at(dz, 1), down)

    for hop in range(1, half + 1):
        for dz, far, where in ((-hop, half, right), (hop, ZS - 1 - half, left)):
            if hop <= far:
                slot = at(dz, 0)
                arrive(1, slot)
                if hop < far:
                    onward(1, slot, where)
                onward(1, slot, up)
                onward(1, slot, down)
        for j in range(YH):
            far_right = half - j % 2
            for dz, far, where in ((-hop, far_right, right), (hop, ZS - 1 - far_right, left)):
                if hop <= far:
                    arrive(0, at(dz, j))
                if hop < far:
                    onward(0, at(dz, j), where)
        cross(hop - 1)
        if hop > 1:
            cross(1 - hop)
        if hop == 1:
            locals_[1].wait()
            for dz in zs:
                there = lax.rem(z + dz, ZS)
                push(rows_ref.at[there], staged.at[there], local_sem.at[1], z_sem.at[there], right).wait_recv()
            keep = pltpu.make_async_copy(staged.at[:, y], own_ref.at[:, y], local_sem.at[1])
            keep.start()
            for dy in ys:
                there = lax.rem(y + dy, YH)
                send(staged.at[:, there], own_ref.at[:, y], y_sem.at[y], device(0, dy))
    cross(half)
    for dz in range(1 - half, half + 1):
        arrive(1, at(dz, 2))
    for dy in ys:
        there = lax.rem(y + dy, YH)
        push(staged.at[:, there], own_ref.at[:, there], local_sem.at[1], y_sem.at[there], right).wait_recv()
    for copy in copies:
        copy.wait_send()
    locals_[0].wait()
    keep.wait()


def gather_row(x, rows):
    supers, width_part, span = x.shape
    any_space = pl.BlockSpec(memory_space=pl.ANY)
    return pl.pallas_call(
        gather_row_kernel,
        out_shape=(
            jax.ShapeDtypeStruct((supers, ZS * YH, width_part, span), x.dtype),
            jax.ShapeDtypeStruct(rows.shape, rows.dtype),
        ),
        in_specs=[any_space, any_space],
        out_specs=(any_space, any_space),
        scratch_shapes=[
            pltpu.VMEM(rows.shape, rows.dtype),
            pltpu.SemaphoreType.DMA((2,)),
            pltpu.SemaphoreType.DMA((80,)),
            pltpu.SemaphoreType.DMA((ZS * YH,)),
            pltpu.SemaphoreType.DMA((ZS * YH,)),
            pltpu.SemaphoreType.DMA((ZS,)),
            pltpu.SemaphoreType.DMA((YH,)),
        ],
        compiler_params=pltpu.CompilerParams(collective_id=1, has_side_effects=True),
        name="gather_row",
    )(x, rows)


def spread_row_kernel(x_ref, out_ref, local_sem, send_sem, recv_sem):
    row, col = lax.axis_index("row"), lax.axis_index("col")
    z, y = row // YH, lax.rem(row, YH)
    tall = [(lax.rem(z + j, ZS) * YH + y, col) for j in range(1, ZS)]
    flat = [(z * YH + lax.rem(y + j, YH), col) for j in range(1, YH)]
    greet(tall + flat)
    mine = pltpu.make_async_copy(x_ref, out_ref.at[z, y], local_sem)
    mine.start()
    copies = []

    def send(src, at, where):
        copy = push(src, out_ref.at[at], send_sem.at[len(copies)], recv_sem.at[at], where)
        copy.start()
        copies.append(copy)

    for where in tall + flat:
        send(x_ref, (z, y), where)
    for j in range(1, ZS):
        there = lax.rem(z + ZS - j, ZS)
        push(x_ref, out_ref.at[there, y], local_sem, recv_sem.at[there, y], flat[0]).wait_recv()
        for where in flat:
            send(out_ref.at[there, y], (there, y), where)
    for j in range(1, YH):
        lane = lax.rem(y + j, YH)
        for i in range(ZS):
            there = lax.rem(z + i, ZS)
            push(x_ref, out_ref.at[there, lane], local_sem, recv_sem.at[there, lane], flat[0]).wait_recv()
    for copy in copies:
        copy.wait_send()
    mine.wait()


def spread_row(x, ident):
    return pl.pallas_call(
        spread_row_kernel,
        out_shape=jax.ShapeDtypeStruct((ZS, YH) + x.shape, x.dtype),
        in_specs=[pl.BlockSpec(memory_space=pl.ANY)],
        out_specs=pl.BlockSpec(memory_space=pl.ANY),
        scratch_shapes=[
            pltpu.SemaphoreType.DMA,
            pltpu.SemaphoreType.DMA((ZS * YH - 1,)),
            pltpu.SemaphoreType.DMA((ZS, YH)),
        ],
        compiler_params=pltpu.CompilerParams(collective_id=ident, has_side_effects=True),
        name="spread_row",
    )(x)


def swap_core_kernel(x_ref, out_ref, send_sem, recv_sem):
    row, col = lax.axis_index("row"), lax.axis_index("col")
    chip, core = col // 2, lax.rem(col, 2)
    partner = (row, chip * 2 + 1 - core)
    greet([partner])
    copy = push(x_ref.at[:, 1 - core], out_ref, send_sem, recv_sem, partner)
    copy.start()
    copy.wait()


def swap_core(x, ident):
    return pl.pallas_call(
        swap_core_kernel,
        out_shape=jax.ShapeDtypeStruct(x.shape[:1] + x.shape[2:], x.dtype),
        in_specs=[pl.BlockSpec(memory_space=pl.ANY)],
        out_specs=pl.BlockSpec(memory_space=pl.ANY),
        scratch_shapes=[pltpu.SemaphoreType.DMA, pltpu.SemaphoreType.DMA],
        compiler_params=pltpu.CompilerParams(collective_id=ident, has_side_effects=True),
        name="swap_core_%d" % ident,
    )(x)


def swap_chips_kernel(x_ref, out_ref, relay, local_sem, send_sem, away_sem, turn_sem, relay_sem, half_sem, recv_sem):
    row, core, at = ring_position()
    chip = at(0, 0)
    rows = x_ref.shape[1]
    cut = rows // 16 * 8
    parts = (pl.ds(0, cut), pl.ds(cut, rows - cut))
    sizes = (cut, rows - cut)

    def device(step):
        return (row, at(*step) * 2 + core)

    greet([device(step) for step in NEAR])
    mine = pltpu.make_async_copy(x_ref.at[chip], out_ref.at[chip], local_sem)
    mine.start()
    copies = []

    def send(src, dst, sem, landing, device):
        copy = push(src, dst, sem, landing, device)
        copy.start()
        copies.append(copy)

    def held(j, dy):
        return relay.at[j, dy, pl.ds(0, sizes[j])]

    for dy in range(2):
        for j in range(2):
            send(x_ref.at[at(2, dy), parts[j]], held(j, dy), away_sem.at[j, dy], relay_sem.at[j, dy], device(NEAR[j]))
    for j, step in enumerate(NEAR):
        send(x_ref.at[at(*step)], out_ref.at[chip], send_sem.at[j], recv_sem.at[chip], device(step))
    for dy in range(2):
        for j in range(2):
            origin = at(XS - NEAR[j][0], 0)
            push(held(j, dy), held(j, dy), local_sem, relay_sem.at[j, dy], device(NEAR[j])).wait_recv()
            target = device((NEAR[j][0], dy))
            send(held(j, dy), out_ref.at[origin, parts[j]], turn_sem.at[j, dy], half_sem.at[j, dy], target)
    for step in NEAR:
        other = at(*step)
        push(x_ref.at[other], out_ref.at[other], local_sem, recv_sem.at[other], device(step)).wait_recv()
    for dy in range(2):
        for j in range(2):
            piece = out_ref.at[at(2, dy), parts[j]]
            push(piece, piece, local_sem, half_sem.at[j, dy], device(NEAR[0])).wait_recv()
    for copy in copies:
        copy.wait_send()
    mine.wait()


def swap_chips(x, ident):
    chips, rows, lanes = x.shape
    four = pltpu.SemaphoreType.DMA((2, 2))
    return pl.pallas_call(
        swap_chips_kernel,
        out_shape=jax.ShapeDtypeStruct(x.shape, x.dtype),
        in_specs=[pl.BlockSpec(memory_space=pl.ANY)],
        out_specs=pl.BlockSpec(memory_space=pl.ANY),
        scratch_shapes=[
            pltpu.VMEM((2, 2, rows - rows // 16 * 8, lanes), x.dtype),
            pltpu.SemaphoreType.DMA,
            pltpu.SemaphoreType.DMA((len(NEAR),)),
            four,
            four,
            four,
            four,
            pltpu.SemaphoreType.DMA((chips,)),
        ],
        compiler_params=pltpu.CompilerParams(collective_id=ident, has_side_effects=True),
        name="swap_chips_%d" % ident,
    )(x)


def swap_row_kernel(along_z, x_ref, out_ref, local_sem, send_sem, recv_sem):
    row, col = lax.axis_index("row"), lax.axis_index("col")
    z, y = row // YH, lax.rem(row, YH)
    count = x_ref.shape[0]
    me = z if along_z else y
    others = [lax.rem(me + j, count) for j in range(1, count)]
    devices = [(other * YH + y if along_z else z * YH + other, col) for other in others]
    greet(devices)
    mine = pltpu.make_async_copy(x_ref.at[me], out_ref.at[me], local_sem)
    mine.start()
    copies = [
        push(x_ref.at[other], out_ref.at[me], send_sem.at[j], recv_sem.at[me], devices[j])
        for j, other in enumerate(others)
    ]
    for copy in copies:
        copy.start()
    for j, other in enumerate(others):
        push(x_ref.at[other], out_ref.at[other], send_sem.at[j], recv_sem.at[other], devices[j]).wait_recv()
    for copy in copies:
        copy.wait_send()
    mine.wait()


def swap_row(x, along_z, ident):
    count = x.shape[0]

    def kernel(*refs):
        swap_row_kernel(along_z, *refs)

    return pl.pallas_call(
        kernel,
        out_shape=jax.ShapeDtypeStruct(x.shape, x.dtype),
        in_specs=[pl.BlockSpec(memory_space=pl.ANY)],
        out_specs=pl.BlockSpec(memory_space=pl.ANY),
        scratch_shapes=[
            pltpu.SemaphoreType.DMA,
            pltpu.SemaphoreType.DMA((count - 1,)),
            pltpu.SemaphoreType.DMA((count,)),
        ],
        compiler_params=pltpu.CompilerParams(collective_id=ident, has_side_effects=True),
        name="swap_row_%d" % ident,
    )(x)


def sum_row(x, ident):
    rows, lanes = x.shape
    piece = jnp.sum(swap_row(x.reshape(YH, rows // YH, lanes), False, ident), axis=0)
    piece = piece.reshape(ZS, rows // (YH * ZS), lanes)
    piece = jnp.sum(swap_row(piece, True, ident + 1), axis=0)
    whole = spread_row(piece, ident + 2)
    return jnp.transpose(whole, (1, 0, 2, 3)).reshape(rows, lanes)


def scatter_sum(x, core, ident):
    grid = x.reshape((CHIPS, 2) + x.shape[1:])
    other = swap_core(grid, ident)
    own = lax.dynamic_index_in_dim(grid, core, 1, keepdims=False)
    return jnp.sum(swap_chips(own + other, ident + 1), axis=0)


def place_kernel(row_block_ref, occupancy_ref, column_ref, blocks_ref, placed_ref, part_ref):
    supers, nblocks = placed_ref.shape[:2]
    per = blocks_ref.shape[2]
    for s in range(supers):

        def step(device, carry, s=s):
            for k in range(per):
                b = device * per + k
                block = blocks_ref[device, s, k]
                keep = occupancy_ref[s, b] > 0
                placed_ref[s, row_block_ref[s, b]] = jnp.where(keep, block, jnp.zeros_like(block))
            return carry

        lax.fori_loop(0, nblocks // per, step, 0)
    first = column_ref[0] * per
    for s in range(supers):
        for k in range(per):
            part_ref[s, :, k * 128 : (k + 1) * 128] = placed_ref[s, first + k]


def place(blocks, occupancy, row_block, column):
    devices, supers, per, width_part, tall = blocks.shape
    smem = pl.BlockSpec(memory_space=pltpu.SMEM)
    vmem = pl.BlockSpec(memory_space=pltpu.VMEM)
    return pl.pallas_call(
        place_kernel,
        out_shape=(
            jax.ShapeDtypeStruct((supers, devices * per, width_part, tall), blocks.dtype),
            jax.ShapeDtypeStruct((supers, width_part, per * tall), blocks.dtype),
        ),
        in_specs=[smem, smem, smem, vmem],
        out_specs=(vmem, vmem),
        name="place",
    )(row_block, occupancy, column.reshape(1).astype(jnp.int32), blocks)


def dot_high(a, b):
    return jnp.dot(a, b, precision=highest)


def per_device(inverse_block, factor_cols, occupancy, row_block, coupling, diag_inverse):
    column = lax.axis_index("col")
    core = lax.rem(column, 2)
    row_parts = lax.axis_size("row")
    col_parts = lax.axis_size("col")
    local_rows = inverse_block.shape[0]
    rows_total = local_rows * row_parts
    supers, span, width_part = factor_cols.shape
    width = width_part * row_parts
    tile = local_rows // col_parts
    diag_cols = diag_inverse.shape[2]
    per = span // 128

    packed = jnp.transpose(factor_cols.reshape(supers, per, 128, width_part), (0, 1, 3, 2))
    placed, part = place(gather_col(packed), occupancy, row_block, column)

    per_row = local_rows // 128
    block_at = jnp.minimum(column * tile // 128, per_row - 2)
    near = lax.dynamic_slice_in_dim(
        placed.reshape(supers, row_parts, per_row, width_part, 128), block_at, 2, 2
    )
    near = jnp.transpose(near, (0, 1, 3, 2, 4)).reshape(supers, row_parts, width_part, 256)
    outgoing = lax.dynamic_slice_in_dim(near, column * tile - block_at * 128, tile, 3)
    outgoing = jnp.transpose(outgoing, (1, 0, 2, 3)).reshape(ZS, YH, -1, 128)
    panel, arrived = gather_row(part, outgoing)
    panel = panel.reshape(supers * width, span)
    arrived = jnp.transpose(arrived.reshape(row_parts, supers, width_part, tile), (1, 0, 2, 3))
    own_rows = arrived.reshape(supers, width, tile).astype(jnp.float32)

    term = lax.dot_general(
        inverse_block, panel, (((1,), (1,)), ((), ())), preferred_element_type=jnp.float32
    )
    summed = scatter_sum(term.reshape(col_parts, tile, supers * width), core, 2)

    columns = []
    chain = []
    here = (jnp.arange(col_parts) == column) & (lax.axis_index("row") == 0)
    here = here.astype(jnp.float32)[:, None, None]
    for s in range(supers):
        product = summed[:, s * width : (s + 1) * width]
        own = own_rows[s]
        if s == 0:
            current = -product
            inner = dot_high(current.T, own.T)
        else:
            link = coupling[s - 1].astype(jnp.float32)
            coupled = dot_high(columns[-1], link)
            current = -(product + coupled)
            inner = dot_high(current.T, own.T) - dot_high(own, coupled)
        embedded = (here * diag_inverse[s].T[None]).reshape(width, width)
        total = embedded - inner / rows_total
        if s > 0:
            total = total + dot_high(link.T, dot_high(chain[-1], link))
        columns.append(current)
        chain.append(total)
    partial = jnp.stack([t.reshape(col_parts, diag_cols, width) for t in chain], axis=1)
    mine = scatter_sum(partial.reshape(col_parts, supers * diag_cols, width), core, 4)
    diagonals = jnp.transpose(sum_row(mine, 6).reshape(supers, diag_cols, width), (0, 2, 1))
    return (jnp.stack(columns), diagonals)


def solution(mesh):
    in_specs = (P("row", "col"), P(None, "col", "row"), P(), P(), P(), P(None, None, "col"))
    out_specs = (P(None, ("row", "col"), None), P(None, None, "col"))
    return jax.shard_map(
        per_device, mesh=mesh, in_specs=in_specs, out_specs=out_specs, check_vma=False
    )
```

```python
import jax
import jax.numpy as jnp
from jax import lax
from jax.experimental import pallas as pl
from jax.experimental.pallas import tpu as pltpu
from jax.sharding import PartitionSpec as P

highest = lax.Precision.HIGHEST
MESH = pl.DeviceIdType.MESH
GRANT = 16 << 20
ZS, YH = 8, 4
CHIPS, XS = 8, 4


def greet(peers):
    barrier = pltpu.get_barrier_semaphore()
    for peer in peers:
        pl.semaphore_signal(barrier, inc=1, device_id=peer, device_id_type=MESH)
    pl.semaphore_wait(barrier, len(peers))


def push(src, dst, send_sem, recv_sem, device):
    return pltpu.make_async_remote_copy(
        src_ref=src,
        dst_ref=dst,
        send_sem=send_sem,
        recv_sem=recv_sem,
        device_id=device,
        device_id_type=MESH,
    )


def ring_position():
    row, col = lax.axis_index("row"), lax.axis_index("col")
    chip, core = col // 2, lax.rem(col, 2)
    x, y = lax.rem(chip, XS), chip // XS

    def at(dx, dy):
        return (y if dy == 0 else 1 - y) * XS + lax.rem(x + dx, XS)

    return row, core, at


NEAR = ((1, 0), (XS - 1, 0), (0, 1), (1, 1), (XS - 1, 1))


def gather_col_kernel(x_ref, out_ref, local_sem, send_sem, pass_sem, turn_sem, half_sem, recv_sem):
    row, core, at = ring_position()
    chip = at(0, 0)
    col = chip * 2 + core
    partner = (row, chip * 2 + 1 - core)
    half = x_ref.shape[0] // 2
    parts = (pl.ds(0, half), pl.ds(half, x_ref.shape[0] - half))
    greet([(row, at(*step) * 2 + core) for step in NEAR] + [partner])
    mine = pltpu.make_async_copy(x_ref, out_ref.at[col], local_sem)
    mine.start()
    copies = []

    def send(src, dst, sem, landing, device):
        copy = push(src, dst, sem, landing, device)
        copy.start()
        copies.append(copy)

    for j, step in enumerate(NEAR):
        send(x_ref, out_ref.at[col], send_sem.at[j], recv_sem.at[col], (row, at(*step) * 2 + core))
    send(x_ref, out_ref.at[col], pass_sem.at[0], recv_sem.at[col], partner)
    for j, step in enumerate(NEAR):
        slot = at(*step) * 2 + core
        push(x_ref, out_ref.at[slot], local_sem, recv_sem.at[slot], partner).wait_recv()
        if step[1] == 0:
            piece = out_ref.at[slot, parts[j]]
            for dy in range(2):
                device = (row, at(XS - step[0], dy) * 2 + core)
                send(piece, piece, turn_sem.at[j, dy], half_sem.at[j, dy], device)
        send(out_ref.at[slot], out_ref.at[slot], pass_sem.at[1 + j], recv_sem.at[slot], partner)
    for dy in range(2):
        slot = at(2, dy) * 2 + core
        for j in range(2):
            piece = out_ref.at[slot, parts[j]]
            push(piece, piece, local_sem, half_sem.at[j, dy], partner).wait_recv()
        send(out_ref.at[slot], out_ref.at[slot], pass_sem.at[6 + dy], recv_sem.at[slot], partner)
    for step in ((0, 0),) + NEAR + ((2, 0), (2, 1)):
        slot = at(*step) * 2 + 1 - core
        push(x_ref, out_ref.at[slot], local_sem, recv_sem.at[slot], partner).wait_recv()
    for copy in copies:
        copy.wait_send()
    mine.wait()


def gather_col(x):
    return pl.pallas_call(
        gather_col_kernel,
        out_shape=jax.ShapeDtypeStruct((CHIPS * 2,) + x.shape, x.dtype),
        in_specs=[pl.BlockSpec(memory_space=pl.ANY)],
        out_specs=pl.BlockSpec(memory_space=pl.ANY),
        scratch_shapes=[
            pltpu.SemaphoreType.DMA,
            pltpu.SemaphoreType.DMA((len(NEAR),)),
            pltpu.SemaphoreType.DMA((CHIPS,)),
            pltpu.SemaphoreType.DMA((2, 2)),
            pltpu.SemaphoreType.DMA((2, 2)),
            pltpu.SemaphoreType.DMA((CHIPS * 2,)),
        ],
        compiler_params=pltpu.CompilerParams(collective_id=0, has_side_effects=True, vmem_limit_bytes=GRANT),
        name="gather_col",
    )(x)


def gather_row_kernel(x_ref, rows_ref, out_ref, own_ref, staged, local_sem, send_sem, wide_sem, thin_sem, z_sem, y_sem):
    row, col = lax.axis_index("row"), lax.axis_index("col")
    z, y = row // YH, lax.rem(row, YH)
    last = x_ref.shape[0] - 1
    parts = (pl.ds(0, last), pl.ds(last, 1))
    sems = (wide_sem, thin_sem)

    def at(dz, dy):
        return lax.rem(z + dz + ZS, ZS) * YH + lax.rem(y + dy + YH, YH)

    def device(dz, dy):
        return (at(dz, dy), col)

    zs, ys = range(1, ZS), range(1, YH)
    greet([device(dz, 0) for dz in zs] + [device(0, dy) for dy in ys])
    locals_ = [pltpu.make_async_copy(x_ref, out_ref.at[:, row], local_sem.at[0])]
    locals_.append(pltpu.make_async_copy(rows_ref.at[z], staged.at[z], local_sem.at[1]))
    for copy in locals_:
        copy.start()
    copies = []

    def send(src, dst, landing, where):
        copy = push(src, dst, send_sem.at[len(copies)], landing, where)
        copy.start()
        copies.append(copy)

    def block(kind, slot):
        return out_ref.at[parts[kind], slot]

    def onward(kind, slot, where, first=False):
        src = x_ref.at[parts[kind]] if first else block(kind, slot)
        send(src, block(kind, slot), sems[kind].at[slot], where)

    def arrive(kind, slot):
        piece = block(kind, slot)
        push(piece, piece, local_sem.at[0], sems[kind].at[slot], device(1, 0)).wait_recv()

    right, left, up, down = device(1, 0), device(-1, 0), device(0, 1), device(0, -1)
    for where in (right, left):
        onward(1, row, where, True)
    for where in (up, down):
        onward(0, row, where, True)
    for where in (right, left):
        onward(0, row, where, True)
    for where in (up, down):
        onward(1, row, where, True)
    for dz in zs:
        there = lax.rem(z + dz, ZS)
        send(rows_ref.at[there], staged.at[z], z_sem.at[z], device(dz, 0))

    for dy in (-1, 1, 2):
        slot = at(0, dy)
        arrive(0, slot)
        if dy == -1:
            onward(0, slot, up)
        onward(0, slot, right)
        onward(0, slot, left)

    half = ZS // 2

    def cross(dz):
        arrive(1, at(dz, -1))
        if dz % 2 == 0:
            onward(1, at(dz, -1), up)
        arrive(1, at(dz, 1))
        if dz % 2 == 1:
            onward(1, at(dz, 1), down)

    for hop in range(1, half + 1):
        for dz, far, where in ((-hop, half, right), (hop, ZS - 1 - half, left)):
            if hop <= far:
                slot = at(dz, 0)
                arrive(1, slot)
                if hop < far:
                    onward(1, slot, where)
                onward(1, slot, up)
                onward(1, slot, down)
        for j in range(YH):
            far_right = half - j % 2
            for dz, far, where in ((-hop, far_right, right), (hop, ZS - 1 - far_right, left)):
                if hop <= far:
                    arrive(0, at(dz, j))
                if hop < far:
                    onward(0, at(dz, j), where)
        cross(hop - 1)
        if hop > 1:
            cross(1 - hop)
        if hop == 1:
            locals_[1].wait()
            for dz in zs:
                there = lax.rem(z + dz, ZS)
                push(rows_ref.at[there], staged.at[there], local_sem.at[1], z_sem.at[there], right).wait_recv()
            keep = pltpu.make_async_copy(staged.at[:, y], own_ref.at[:, y], local_sem.at[1])
            keep.start()
            for dy in ys:
                there = lax.rem(y + dy, YH)
                send(staged.at[:, there], own_ref.at[:, y], y_sem.at[y], device(0, dy))
    cross(half)
    for dz in range(1 - half, half + 1):
        arrive(1, at(dz, 2))
    for dy in ys:
        there = lax.rem(y + dy, YH)
        push(staged.at[:, there], own_ref.at[:, there], local_sem.at[1], y_sem.at[there], right).wait_recv()
    for copy in copies:
        copy.wait_send()
    locals_[0].wait()
    keep.wait()


def gather_row(x, rows):
    supers, width_part, span = x.shape
    any_space = pl.BlockSpec(memory_space=pl.ANY)
    return pl.pallas_call(
        gather_row_kernel,
        out_shape=(
            jax.ShapeDtypeStruct((supers, ZS * YH, width_part, span), x.dtype),
            jax.ShapeDtypeStruct(rows.shape, rows.dtype),
        ),
        in_specs=[any_space, any_space],
        out_specs=(any_space, any_space),
        scratch_shapes=[
            pltpu.VMEM(rows.shape, rows.dtype),
            pltpu.SemaphoreType.DMA((2,)),
            pltpu.SemaphoreType.DMA((80,)),
            pltpu.SemaphoreType.DMA((ZS * YH,)),
            pltpu.SemaphoreType.DMA((ZS * YH,)),
            pltpu.SemaphoreType.DMA((ZS,)),
            pltpu.SemaphoreType.DMA((YH,)),
        ],
        compiler_params=pltpu.CompilerParams(collective_id=1, has_side_effects=True, vmem_limit_bytes=GRANT),
        name="gather_row",
    )(x, rows)


def spread_row_kernel(x_ref, out_ref, local_sem, send_sem, recv_sem):
    row, col = lax.axis_index("row"), lax.axis_index("col")
    z, y = row // YH, lax.rem(row, YH)
    tall = [(lax.rem(z + j, ZS) * YH + y, col) for j in range(1, ZS)]
    flat = [(z * YH + lax.rem(y + j, YH), col) for j in range(1, YH)]
    greet(tall + flat)
    mine = pltpu.make_async_copy(x_ref, out_ref.at[z, y], local_sem)
    mine.start()
    copies = []

    def send(src, at, where):
        copy = push(src, out_ref.at[at], send_sem.at[len(copies)], recv_sem.at[at], where)
        copy.start()
        copies.append(copy)

    for where in tall + flat:
        send(x_ref, (z, y), where)
    for j in range(1, ZS):
        there = lax.rem(z + ZS - j, ZS)
        push(x_ref, out_ref.at[there, y], local_sem, recv_sem.at[there, y], flat[0]).wait_recv()
        for where in flat:
            send(out_ref.at[there, y], (there, y), where)
    for j in range(1, YH):
        lane = lax.rem(y + j, YH)
        for i in range(ZS):
            there = lax.rem(z + i, ZS)
            push(x_ref, out_ref.at[there, lane], local_sem, recv_sem.at[there, lane], flat[0]).wait_recv()
    for copy in copies:
        copy.wait_send()
    mine.wait()


def spread_row(x, ident):
    return pl.pallas_call(
        spread_row_kernel,
        out_shape=jax.ShapeDtypeStruct((ZS, YH) + x.shape, x.dtype),
        in_specs=[pl.BlockSpec(memory_space=pl.ANY)],
        out_specs=pl.BlockSpec(memory_space=pl.ANY),
        scratch_shapes=[
            pltpu.SemaphoreType.DMA,
            pltpu.SemaphoreType.DMA((ZS * YH - 1,)),
            pltpu.SemaphoreType.DMA((ZS, YH)),
        ],
        compiler_params=pltpu.CompilerParams(collective_id=ident, has_side_effects=True, vmem_limit_bytes=GRANT),
        name="spread_row",
    )(x)


def swap_core_kernel(x_ref, out_ref, got, send_sem, recv_sem):
    row, col = lax.axis_index("row"), lax.axis_index("col")
    chip, core = col // 2, lax.rem(col, 2)
    partner = (row, chip * 2 + 1 - core)
    greet([partner])
    copy = push(x_ref.at[:, 1 - core], got, send_sem, recv_sem, partner)
    copy.start()
    copy.wait()

    def add(i, carry):
        rows = pl.ds(pl.multiple_of(i * 8, 8), 8)
        for j in range(CHIPS):
            out_ref[j, rows] = x_ref[j, core, rows] + got[j, rows]
        return carry

    lax.fori_loop(0, x_ref.shape[2] // 8, add, 0)


def swap_core(x, ident):
    shape = x.shape[:1] + x.shape[2:]
    return pl.pallas_call(
        swap_core_kernel,
        out_shape=jax.ShapeDtypeStruct(shape, x.dtype),
        in_specs=[pl.BlockSpec(memory_space=pltpu.VMEM)],
        out_specs=pl.BlockSpec(memory_space=pltpu.VMEM),
        scratch_shapes=[pltpu.VMEM(shape, x.dtype), pltpu.SemaphoreType.DMA, pltpu.SemaphoreType.DMA],
        compiler_params=pltpu.CompilerParams(collective_id=ident, has_side_effects=True, vmem_limit_bytes=GRANT),
        name="swap_core_%d" % ident,
    )(x)


def swap_chips_kernel(x_ref, sum_ref, out_ref, relay, local_sem, send_sem, away_sem, turn_sem, relay_sem, half_sem, recv_sem):
    row, core, at = ring_position()
    chip = at(0, 0)
    rows = x_ref.shape[1]
    cut = rows // 16 * 8
    parts = (pl.ds(0, cut), pl.ds(cut, rows - cut))
    sizes = (cut, rows - cut)

    def device(step):
        return (row, at(*step) * 2 + core)

    greet([device(step) for step in NEAR])
    copies = []

    def send(src, dst, sem, landing, device):
        copy = push(src, dst, sem, landing, device)
        copy.start()
        copies.append(copy)

    def held(j, dy):
        return relay.at[j, dy, pl.ds(0, sizes[j])]

    for dy in range(2):
        for j in range(2):
            send(x_ref.at[at(2, dy), parts[j]], held(j, dy), away_sem.at[j, dy], relay_sem.at[j, dy], device(NEAR[j]))
    for j, step in enumerate(NEAR):
        send(x_ref.at[at(*step)], out_ref.at[chip], send_sem.at[j], recv_sem.at[chip], device(step))
    for dy in range(2):
        for j in range(2):
            origin = at(XS - NEAR[j][0], 0)
            push(held(j, dy), held(j, dy), local_sem, relay_sem.at[j, dy], device(NEAR[j])).wait_recv()
            target = device((NEAR[j][0], dy))
            send(held(j, dy), out_ref.at[origin, parts[j]], turn_sem.at[j, dy], half_sem.at[j, dy], target)
    for step in NEAR:
        other = at(*step)
        push(x_ref.at[other], out_ref.at[other], local_sem, recv_sem.at[other], device(step)).wait_recv()
    for dy in range(2):
        for j in range(2):
            piece = out_ref.at[at(2, dy), parts[j]]
            push(piece, piece, local_sem, half_sem.at[j, dy], device(NEAR[0])).wait_recv()
    others = [at(*step) for step in NEAR + ((2, 0), (2, 1))]

    def add(i, carry):
        span = pl.ds(pl.multiple_of(i * 8, 8), 8)
        total = x_ref[chip, span]
        for other in others:
            total = total + out_ref[other, span]
        sum_ref[span] = total
        return carry

    lax.fori_loop(0, rows // 8, add, 0)
    for copy in copies:
        copy.wait_send()


def swap_chips(x, ident):
    chips, rows, lanes = x.shape
    four = pltpu.SemaphoreType.DMA((2, 2))
    return pl.pallas_call(
        swap_chips_kernel,
        out_shape=jax.ShapeDtypeStruct(x.shape[1:], x.dtype),
        in_specs=[pl.BlockSpec(memory_space=pltpu.VMEM)],
        out_specs=pl.BlockSpec(memory_space=pltpu.VMEM),
        scratch_shapes=[
            pltpu.VMEM(x.shape, x.dtype),
            pltpu.VMEM((2, 2, rows - rows // 16 * 8, lanes), x.dtype),
            pltpu.SemaphoreType.DMA,
            pltpu.SemaphoreType.DMA((len(NEAR),)),
            four,
            four,
            four,
            four,
            pltpu.SemaphoreType.DMA((chips,)),
        ],
        compiler_params=pltpu.CompilerParams(collective_id=ident, has_side_effects=True, vmem_limit_bytes=GRANT),
        name="swap_chips_%d" % ident,
    )(x)


def swap_row_kernel(along_z, x_ref, sum_ref, out_ref, send_sem, recv_sem):
    row, col = lax.axis_index("row"), lax.axis_index("col")
    z, y = row // YH, lax.rem(row, YH)
    count = x_ref.shape[0]
    me = z if along_z else y
    others = [lax.rem(me + j, count) for j in range(1, count)]
    devices = [(other * YH + y if along_z else z * YH + other, col) for other in others]
    greet(devices)
    copies = [
        push(x_ref.at[other], out_ref.at[me], send_sem.at[j], recv_sem.at[me], devices[j])
        for j, other in enumerate(others)
    ]
    for copy in copies:
        copy.start()
    for j, other in enumerate(others):
        push(x_ref.at[other], out_ref.at[other], send_sem.at[j], recv_sem.at[other], devices[j]).wait_recv()
    total = x_ref[me]
    for other in others:
        total = total + out_ref[other]
    sum_ref[...] = total
    for copy in copies:
        copy.wait_send()


def swap_row(x, along_z, ident):
    count = x.shape[0]

    def kernel(*refs):
        swap_row_kernel(along_z, *refs)

    return pl.pallas_call(
        kernel,
        out_shape=jax.ShapeDtypeStruct(x.shape[1:], x.dtype),
        in_specs=[pl.BlockSpec(memory_space=pltpu.VMEM)],
        out_specs=pl.BlockSpec(memory_space=pltpu.VMEM),
        scratch_shapes=[
            pltpu.VMEM(x.shape, x.dtype),
            pltpu.SemaphoreType.DMA((count - 1,)),
            pltpu.SemaphoreType.DMA((count,)),
        ],
        compiler_params=pltpu.CompilerParams(collective_id=ident, has_side_effects=True, vmem_limit_bytes=GRANT),
        name="swap_row_%d" % ident,
    )(x)


def sum_row(x, ident):
    rows, lanes = x.shape
    piece = swap_row(x.reshape(YH, rows // YH, lanes), False, ident)
    piece = piece.reshape(ZS, rows // (YH * ZS), lanes)
    piece = swap_row(piece, True, ident + 1)
    whole = spread_row(piece, ident + 2)
    return jnp.transpose(whole, (1, 0, 2, 3)).reshape(rows, lanes)


def scatter_sum(x, ident):
    return swap_chips(swap_core(x.reshape((CHIPS, 2) + x.shape[1:]), ident), ident + 1)


def place_kernel(row_block_ref, occupancy_ref, column_ref, blocks_ref, placed_ref, part_ref):
    supers, nblocks = placed_ref.shape[:2]
    per = blocks_ref.shape[2]
    for s in range(supers):

        def step(device, carry, s=s):
            for k in range(per):
                b = device * per + k
                block = blocks_ref[device, s, k]
                keep = occupancy_ref[s, b] > 0
                placed_ref[s, row_block_ref[s, b]] = jnp.where(keep, block, jnp.zeros_like(block))
            return carry

        lax.fori_loop(0, nblocks // per, step, 0)
    first = column_ref[0] * per
    for s in range(supers):
        for k in range(per):
            part_ref[s, :, k * 128 : (k + 1) * 128] = placed_ref[s, first + k]


def place(blocks, occupancy, row_block, column):
    devices, supers, per, width_part, tall = blocks.shape
    smem = pl.BlockSpec(memory_space=pltpu.SMEM)
    vmem = pl.BlockSpec(memory_space=pltpu.VMEM)
    return pl.pallas_call(
        place_kernel,
        out_shape=(
            jax.ShapeDtypeStruct((supers, devices * per, width_part, tall), blocks.dtype),
            jax.ShapeDtypeStruct((supers, width_part, per * tall), blocks.dtype),
        ),
        in_specs=[smem, smem, smem, vmem],
        out_specs=(vmem, vmem),
        compiler_params=pltpu.CompilerParams(vmem_limit_bytes=GRANT),
        name="place",
    )(row_block, occupancy, column.reshape(1).astype(jnp.int32), blocks)


def dot_high(a, b):
    return jnp.dot(a, b, precision=highest)


def per_device(inverse_block, factor_cols, occupancy, row_block, coupling, diag_inverse):
    column = lax.axis_index("col")
    row_parts = lax.axis_size("row")
    col_parts = lax.axis_size("col")
    local_rows = inverse_block.shape[0]
    rows_total = local_rows * row_parts
    supers, span, width_part = factor_cols.shape
    width = width_part * row_parts
    tile = local_rows // col_parts
    diag_cols = diag_inverse.shape[2]
    per = span // 128

    packed = jnp.transpose(factor_cols.reshape(supers, per, 128, width_part), (0, 1, 3, 2))
    placed, part = place(gather_col(packed), occupancy, row_block, column)

    per_row = local_rows // 128
    block_at = jnp.minimum(column * tile // 128, per_row - 2)
    near = lax.dynamic_slice_in_dim(
        placed.reshape(supers, row_parts, per_row, width_part, 128), block_at, 2, 2
    )
    near = jnp.transpose(near, (0, 1, 3, 2, 4)).reshape(supers, row_parts, width_part, 256)
    outgoing = lax.dynamic_slice_in_dim(near, column * tile - block_at * 128, tile, 3)
    outgoing = jnp.transpose(outgoing, (1, 0, 2, 3)).reshape(ZS, YH, -1, 128)
    panel, arrived = gather_row(part, outgoing)
    panel = panel.reshape(supers * width, span)
    arrived = jnp.transpose(arrived.reshape(row_parts, supers, width_part, tile), (1, 0, 2, 3))
    own_rows = arrived.reshape(supers, width, tile).astype(jnp.float32)

    term = lax.dot_general(
        inverse_block, panel, (((1,), (1,)), ((), ())), preferred_element_type=jnp.float32
    )
    summed = scatter_sum(term.reshape(col_parts, tile, supers * width), 2)

    columns = []
    chain = []
    here = (jnp.arange(col_parts) == column) & (lax.axis_index("row") == 0)
    here = here.astype(jnp.float32)[:, None, None]
    for s in range(supers):
        product = summed[:, s * width : (s + 1) * width]
        own = own_rows[s]
        if s == 0:
            current = -product
            inner = dot_high(current.T, own.T)
        else:
            link = coupling[s - 1].astype(jnp.float32)
            coupled = dot_high(columns[-1], link)
            current = -(product + coupled)
            inner = dot_high(current.T, own.T) - dot_high(own, coupled)
        embedded = (here * diag_inverse[s].T[None]).reshape(width, width)
        total = embedded - inner / rows_total
        if s > 0:
            total = total + dot_high(link.T, dot_high(chain[-1], link))
        columns.append(current)
        chain.append(total)
    partial = jnp.stack([t.reshape(col_parts, diag_cols, width) for t in chain], axis=1)
    mine = scatter_sum(partial.reshape(col_parts, supers * diag_cols, width), 4)
    diagonals = jnp.transpose(sum_row(mine, 6).reshape(supers, diag_cols, width), (0, 2, 1))
    return (jnp.stack(columns), diagonals)


def solution(mesh):
    in_specs = (P("row", "col"), P(None, "col", "row"), P(), P(), P(), P(None, None, "col"))
    out_specs = (P(None, ("row", "col"), None), P(None, None, "col"))
    return jax.shard_map(
        per_device, mesh=mesh, in_specs=in_specs, out_specs=out_specs, check_vma=False
    )
```

```python
import jax
import jax.numpy as jnp
from jax import lax
from jax.experimental import pallas as pl
from jax.experimental.pallas import tpu as pltpu
from jax.sharding import PartitionSpec as P

highest = lax.Precision.HIGHEST
MESH = pl.DeviceIdType.MESH
GRANT = 16 << 20
ZS, YH = 8, 4
CHIPS, XS = 8, 4


def greet(peers):
    barrier = pltpu.get_barrier_semaphore()
    for peer in peers:
        pl.semaphore_signal(barrier, inc=1, device_id=peer, device_id_type=MESH)
    pl.semaphore_wait(barrier, len(peers))


def push(src, dst, send_sem, recv_sem, device):
    return pltpu.make_async_remote_copy(
        src_ref=src,
        dst_ref=dst,
        send_sem=send_sem,
        recv_sem=recv_sem,
        device_id=device,
        device_id_type=MESH,
    )


def ring_position():
    row, col = lax.axis_index("row"), lax.axis_index("col")
    chip, core = col // 2, lax.rem(col, 2)
    x, y = lax.rem(chip, XS), chip // XS

    def at(dx, dy):
        return (y if dy == 0 else 1 - y) * XS + lax.rem(x + dx, XS)

    return row, core, at


NEAR = ((1, 0), (XS - 1, 0), (0, 1), (1, 1), (XS - 1, 1))


def gather_col_kernel(x_ref, out_ref, local_sem, send_sem, pass_sem, turn_sem, half_sem, recv_sem):
    row, core, at = ring_position()
    chip = at(0, 0)
    col = chip * 2 + core
    partner = (row, chip * 2 + 1 - core)
    half = x_ref.shape[0] // 2
    parts = (pl.ds(0, half), pl.ds(half, x_ref.shape[0] - half))
    greet([(row, at(*step) * 2 + core) for step in NEAR] + [partner])
    mine = pltpu.make_async_copy(x_ref, out_ref.at[col], local_sem)
    mine.start()
    copies = []

    def send(src, dst, sem, landing, device):
        copy = push(src, dst, sem, landing, device)
        copy.start()
        copies.append(copy)

    for j, step in enumerate(NEAR):
        send(x_ref, out_ref.at[col], send_sem.at[j], recv_sem.at[col], (row, at(*step) * 2 + core))
    send(x_ref, out_ref.at[col], pass_sem.at[0], recv_sem.at[col], partner)
    for j, step in enumerate(NEAR):
        slot = at(*step) * 2 + core
        push(x_ref, out_ref.at[slot], local_sem, recv_sem.at[slot], partner).wait_recv()
        if step[1] == 0:
            piece = out_ref.at[slot, parts[j]]
            for dy in range(2):
                device = (row, at(XS - step[0], dy) * 2 + core)
                send(piece, piece, turn_sem.at[j, dy], half_sem.at[j, dy], device)
        send(out_ref.at[slot], out_ref.at[slot], pass_sem.at[1 + j], recv_sem.at[slot], partner)
    for dy in range(2):
        slot = at(2, dy) * 2 + core
        for j in range(2):
            piece = out_ref.at[slot, parts[j]]
            push(piece, piece, local_sem, half_sem.at[j, dy], partner).wait_recv()
        send(out_ref.at[slot], out_ref.at[slot], pass_sem.at[6 + dy], recv_sem.at[slot], partner)
    for step in ((0, 0),) + NEAR + ((2, 0), (2, 1)):
        slot = at(*step) * 2 + 1 - core
        push(x_ref, out_ref.at[slot], local_sem, recv_sem.at[slot], partner).wait_recv()
    for copy in copies:
        copy.wait_send()
    mine.wait()


def gather_col(x):
    return pl.pallas_call(
        gather_col_kernel,
        out_shape=jax.ShapeDtypeStruct((CHIPS * 2,) + x.shape, x.dtype),
        in_specs=[pl.BlockSpec(memory_space=pl.ANY)],
        out_specs=pl.BlockSpec(memory_space=pl.ANY),
        scratch_shapes=[
            pltpu.SemaphoreType.DMA,
            pltpu.SemaphoreType.DMA((len(NEAR),)),
            pltpu.SemaphoreType.DMA((CHIPS,)),
            pltpu.SemaphoreType.DMA((2, 2)),
            pltpu.SemaphoreType.DMA((2, 2)),
            pltpu.SemaphoreType.DMA((CHIPS * 2,)),
        ],
        compiler_params=pltpu.CompilerParams(collective_id=0, has_side_effects=True, vmem_limit_bytes=GRANT),
        name="gather_col",
    )(x)


def gather_row_kernel(x_ref, out_ref, local_sem, send_sem, wide_sem, thin_sem):
    row, col = lax.axis_index("row"), lax.axis_index("col")
    z, y = row // YH, lax.rem(row, YH)
    last = x_ref.shape[0] - 1
    parts = (pl.ds(0, last), pl.ds(last, 1))
    sems = (wide_sem, thin_sem)

    def at(dz, dy):
        return lax.rem(z + dz + ZS, ZS) * YH + lax.rem(y + dy + YH, YH)

    def device(dz, dy):
        return (at(dz, dy), col)

    right, left, up, down = device(1, 0), device(-1, 0), device(0, 1), device(0, -1)
    greet([right, left, up, down])
    mine = pltpu.make_async_copy(x_ref, out_ref.at[:, row], local_sem)
    mine.start()
    copies = []

    def send(src, dst, landing, where):
        copy = push(src, dst, send_sem.at[len(copies)], landing, where)
        copy.start()
        copies.append(copy)

    def block(kind, slot):
        return out_ref.at[parts[kind], slot]

    def onward(kind, slot, where, first=False):
        src = x_ref.at[parts[kind]] if first else block(kind, slot)
        send(src, block(kind, slot), sems[kind].at[slot], where)

    def arrive(kind, slot):
        piece = block(kind, slot)
        push(piece, piece, local_sem, sems[kind].at[slot], right).wait_recv()

    for where in (right, left):
        onward(1, row, where, True)
    for where in (up, down):
        onward(0, row, where, True)
    for where in (right, left):
        onward(0, row, where, True)
    for where in (up, down):
        onward(1, row, where, True)

    for dy in (-1, 1, 2):
        slot = at(0, dy)
        arrive(0, slot)
        if dy == -1:
            onward(0, slot, up)
        onward(0, slot, right)
        onward(0, slot, left)

    half = ZS // 2

    def cross(dz):
        arrive(1, at(dz, -1))
        if dz % 2 == 0:
            onward(1, at(dz, -1), up)
        arrive(1, at(dz, 1))
        if dz % 2 == 1:
            onward(1, at(dz, 1), down)

    for hop in range(1, half + 1):
        for dz, far, where in ((-hop, half, right), (hop, ZS - 1 - half, left)):
            if hop <= far:
                slot = at(dz, 0)
                arrive(1, slot)
                if hop < far:
                    onward(1, slot, where)
                onward(1, slot, up)
                onward(1, slot, down)
        for j in range(YH):
            far_right = half - j % 2
            for dz, far, where in ((-hop, far_right, right), (hop, ZS - 1 - far_right, left)):
                if hop <= far:
                    arrive(0, at(dz, j))
                if hop < far:
                    onward(0, at(dz, j), where)
        cross(hop - 1)
        if hop > 1:
            cross(1 - hop)
    cross(half)
    for dz in range(1 - half, half + 1):
        arrive(1, at(dz, 2))
    for copy in copies:
        copy.wait_send()
    mine.wait()


def gather_row(x):
    supers, width_part, span = x.shape
    return pl.pallas_call(
        gather_row_kernel,
        out_shape=jax.ShapeDtypeStruct((supers, ZS * YH, width_part, span), x.dtype),
        in_specs=[pl.BlockSpec(memory_space=pl.ANY)],
        out_specs=pl.BlockSpec(memory_space=pl.ANY),
        scratch_shapes=[
            pltpu.SemaphoreType.DMA,
            pltpu.SemaphoreType.DMA((80,)),
            pltpu.SemaphoreType.DMA((ZS * YH,)),
            pltpu.SemaphoreType.DMA((ZS * YH,)),
        ],
        compiler_params=pltpu.CompilerParams(collective_id=1, has_side_effects=True, vmem_limit_bytes=GRANT),
        name="gather_row",
    )(x)


def swap_core_kernel(x_ref, out_ref, got, send_sem, recv_sem):
    row, col = lax.axis_index("row"), lax.axis_index("col")
    chip, core = col // 2, lax.rem(col, 2)
    partner = (row, chip * 2 + 1 - core)
    greet([partner])
    copy = push(x_ref.at[:, 1 - core], got, send_sem, recv_sem, partner)
    copy.start()
    copy.wait()

    def add(i, carry):
        rows = pl.ds(pl.multiple_of(i * 8, 8), 8)
        for j in range(CHIPS):
            out_ref[j, rows] = x_ref[j, core, rows] + got[j, rows]
        return carry

    lax.fori_loop(0, x_ref.shape[2] // 8, add, 0)


def swap_core(x, ident):
    shape = x.shape[:1] + x.shape[2:]
    return pl.pallas_call(
        swap_core_kernel,
        out_shape=jax.ShapeDtypeStruct(shape, x.dtype),
        in_specs=[pl.BlockSpec(memory_space=pltpu.VMEM)],
        out_specs=pl.BlockSpec(memory_space=pltpu.VMEM),
        scratch_shapes=[pltpu.VMEM(shape, x.dtype), pltpu.SemaphoreType.DMA, pltpu.SemaphoreType.DMA],
        compiler_params=pltpu.CompilerParams(collective_id=ident, has_side_effects=True, vmem_limit_bytes=GRANT),
        name="swap_core_%d" % ident,
    )(x)


class RowExchange:
    def __init__(self, rows_ref, own_ref, staged, local_sem, send_sem, z_sem, y_sem):
        self.rows, self.own, self.staged = rows_ref, own_ref, staged
        self.local_sem, self.send_sem, self.z_sem, self.y_sem = local_sem, send_sem, z_sem, y_sem
        row, self.col = lax.axis_index("row"), lax.axis_index("col")
        self.z, self.y = row // YH, lax.rem(row, YH)
        self.over_z = [lax.rem(self.z + j, ZS) for j in range(1, ZS)]
        self.over_y = [lax.rem(self.y + j, YH) for j in range(1, YH)]
        self.z_devices = [(other * YH + self.y, self.col) for other in self.over_z]
        self.y_devices = [(self.z * YH + other, self.col) for other in self.over_y]
        self.copies = []

    def send(self, *args):
        copy = push(*args)
        copy.start()
        self.copies.append(copy)

    def begin(self):
        self.mine = pltpu.make_async_copy(self.rows.at[self.z], self.staged.at[self.z], self.local_sem)
        self.mine.start()
        for j, other in enumerate(self.over_z):
            self.send(self.rows.at[other], self.staged.at[self.z], self.send_sem.at[j], self.z_sem.at[self.z], self.z_devices[j])

    def turn(self):
        self.mine.wait()
        for j, other in enumerate(self.over_z):
            push(self.rows.at[other], self.staged.at[other], self.local_sem, self.z_sem.at[other], self.z_devices[j]).wait_recv()
        self.mine = pltpu.make_async_copy(self.staged.at[:, self.y], self.own.at[:, self.y], self.local_sem)
        self.mine.start()
        for j, other in enumerate(self.over_y):
            self.send(self.staged.at[:, other], self.own.at[:, self.y], self.send_sem.at[ZS - 1 + j], self.y_sem.at[self.y], self.y_devices[j])

    def end(self):
        for j, other in enumerate(self.over_y):
            push(self.staged.at[:, other], self.own.at[:, other], self.local_sem, self.y_sem.at[other], self.y_devices[j]).wait_recv()
        for copy in self.copies:
            copy.wait_send()
        self.mine.wait()


def swap_chips_kernel(x_ref, sum_ref, out_ref, relay, local_sem, send_sem, away_sem, turn_sem, relay_sem, half_sem, recv_sem, ride=None):
    row, core, at = ring_position()
    chip = at(0, 0)
    rows = x_ref.shape[1]
    cut = rows // 16 * 8
    parts = (pl.ds(0, cut), pl.ds(cut, rows - cut))
    sizes = (cut, rows - cut)

    def device(step):
        return (row, at(*step) * 2 + core)

    greet([device(step) for step in NEAR] + (ride.z_devices + ride.y_devices if ride else []))
    if ride:
        ride.begin()
    copies = []

    def send(src, dst, sem, landing, device):
        copy = push(src, dst, sem, landing, device)
        copy.start()
        copies.append(copy)

    def held(j, dy):
        return relay.at[j, dy, pl.ds(0, sizes[j])]

    for dy in range(2):
        for j in range(2):
            send(x_ref.at[at(2, dy), parts[j]], held(j, dy), away_sem.at[j, dy], relay_sem.at[j, dy], device(NEAR[j]))
    for j, step in enumerate(NEAR):
        send(x_ref.at[at(*step)], out_ref.at[chip], send_sem.at[j], recv_sem.at[chip], device(step))
    for dy in range(2):
        for j in range(2):
            origin = at(XS - NEAR[j][0], 0)
            push(held(j, dy), held(j, dy), local_sem, relay_sem.at[j, dy], device(NEAR[j])).wait_recv()
            target = device((NEAR[j][0], dy))
            send(held(j, dy), out_ref.at[origin, parts[j]], turn_sem.at[j, dy], half_sem.at[j, dy], target)
    if ride:
        ride.turn()
    for step in NEAR:
        other = at(*step)
        push(x_ref.at[other], out_ref.at[other], local_sem, recv_sem.at[other], device(step)).wait_recv()
    for dy in range(2):
        for j in range(2):
            piece = out_ref.at[at(2, dy), parts[j]]
            push(piece, piece, local_sem, half_sem.at[j, dy], device(NEAR[0])).wait_recv()
    others = [at(*step) for step in NEAR + ((2, 0), (2, 1))]

    def add(i, carry):
        span = pl.ds(pl.multiple_of(i * 8, 8), 8)
        total = x_ref[chip, span]
        for other in others:
            total = total + out_ref[other, span]
        sum_ref[span] = total
        return carry

    lax.fori_loop(0, rows // 8, add, 0)
    for copy in copies:
        copy.wait_send()
    if ride:
        ride.end()


def swap_chips(x, ident, rows=None):
    chips, tall, lanes = x.shape
    dma = pltpu.SemaphoreType.DMA
    shapes = [jax.ShapeDtypeStruct(x.shape[1:], x.dtype)]
    scratch = [
        pltpu.VMEM(x.shape, x.dtype),
        pltpu.VMEM((2, 2, tall - tall // 16 * 8, lanes), x.dtype),
        dma,
        dma((len(NEAR),)),
        dma((2, 2)),
        dma((2, 2)),
        dma((2, 2)),
        dma((2, 2)),
        dma((chips,)),
    ]
    own = len(scratch)
    operands = [x]
    if rows is not None:
        operands.append(rows)
        shapes.append(jax.ShapeDtypeStruct(rows.shape, rows.dtype))
        scratch += [pltpu.VMEM(rows.shape, rows.dtype), dma, dma((ZS + YH - 2,)), dma((ZS,)), dma((YH,))]

    def kernel(*refs):
        count = len(operands)
        arrays, rest = refs[: 2 * count], refs[2 * count :]
        ride = RowExchange(arrays[1], arrays[3], *rest[own:]) if count == 2 else None
        swap_chips_kernel(arrays[0], arrays[count], *rest[:own], ride=ride)

    vmem = pl.BlockSpec(memory_space=pltpu.VMEM)
    return pl.pallas_call(
        kernel,
        out_shape=shapes,
        in_specs=[vmem] * len(operands),
        out_specs=[vmem] * len(operands),
        scratch_shapes=scratch,
        compiler_params=pltpu.CompilerParams(collective_id=ident, has_side_effects=True, vmem_limit_bytes=GRANT),
        name="swap_chips_%d" % ident,
    )(*operands)


def sum_row_kernel(x_ref, out_ref, got_y, mid, got_z, whole, y_send, y_recv, z_send, z_recv, send_sem, recv_sem):
    row, col = lax.axis_index("row"), lax.axis_index("col")
    z, y = row // YH, lax.rem(row, YH)
    zs = [lax.rem(z + j, ZS) for j in range(1, ZS)]
    ys = [lax.rem(y + j, YH) for j in range(1, YH)]
    tall = [(other * YH + y, col) for other in zs]
    flat = [(z * YH + other, col) for other in ys]
    greet(tall + flat)
    copies = []

    def send(*args):
        copy = push(*args)
        copy.start()
        copies.append(copy)

    for j, other in enumerate(ys):
        send(x_ref.at[other], got_y.at[y], y_send.at[j], y_recv.at[y], flat[j])
    for j, other in enumerate(ys):
        push(x_ref.at[other], got_y.at[other], y_send.at[j], y_recv.at[other], flat[j]).wait_recv()
    total = x_ref[y]
    for other in ys:
        total = total + got_y[other]
    mid[...] = total
    for j, other in enumerate(zs):
        send(mid.at[other], got_z.at[z], z_send.at[j], z_recv.at[z], tall[j])
    for j, other in enumerate(zs):
        push(mid.at[other], got_z.at[other], z_send.at[j], z_recv.at[other], tall[j]).wait_recv()
    total = mid[z]
    for other in zs:
        total = total + got_z[other]
    whole[...] = total
    out_ref[z, y] = total
    first = len(copies)

    def spread(src, at, where):
        send(src, out_ref.at[at], send_sem.at[len(copies) - first], recv_sem.at[at], where)

    for where in tall + flat:
        spread(whole, (z, y), where)
    for j in range(1, ZS):
        there = lax.rem(z + ZS - j, ZS)
        push(whole, out_ref.at[there, y], y_send.at[0], recv_sem.at[there, y], flat[0]).wait_recv()
        for where in flat:
            spread(out_ref.at[there, y], (there, y), where)
    for lane in ys:
        for there in [z] + zs:
            push(whole, out_ref.at[there, lane], y_send.at[0], recv_sem.at[there, lane], flat[0]).wait_recv()
    for copy in copies:
        copy.wait_send()


def sum_row(x, ident):
    rows, lanes = x.shape
    grid = x.reshape(YH, ZS, rows // (YH * ZS), lanes)
    dma = pltpu.SemaphoreType.DMA
    vmem = pl.BlockSpec(memory_space=pltpu.VMEM)
    whole = pl.pallas_call(
        sum_row_kernel,
        out_shape=jax.ShapeDtypeStruct((ZS, YH) + grid.shape[2:], x.dtype),
        in_specs=[vmem],
        out_specs=vmem,
        scratch_shapes=[
            pltpu.VMEM(grid.shape, x.dtype),
            pltpu.VMEM(grid.shape[1:], x.dtype),
            pltpu.VMEM(grid.shape[1:], x.dtype),
            pltpu.VMEM(grid.shape[2:], x.dtype),
            dma((YH - 1,)),
            dma((YH,)),
            dma((ZS - 1,)),
            dma((ZS,)),
            dma((ZS * YH - 1,)),
            dma((ZS, YH)),
        ],
        compiler_params=pltpu.CompilerParams(collective_id=ident, has_side_effects=True, vmem_limit_bytes=GRANT),
        name="sum_row",
    )(grid)
    return jnp.transpose(whole, (1, 0, 2, 3)).reshape(rows, lanes)


def scatter_sum(x, ident, rows=None):
    return swap_chips(swap_core(x.reshape((CHIPS, 2) + x.shape[1:]), ident), ident + 1, rows)


def place_kernel(row_block_ref, occupancy_ref, start_ref, blocks_ref, near_ref, part_ref, placed_ref):
    supers, nblocks = placed_ref.shape[:2]
    per = blocks_ref.shape[2]
    for s in range(supers):

        def step(device, carry, s=s):
            for k in range(per):
                b = device * per + k
                block = blocks_ref[device, s, k]
                keep = occupancy_ref[s, b] > 0
                placed_ref[s, row_block_ref[s, b]] = jnp.where(keep, block, jnp.zeros_like(block))
            return carry

        lax.fori_loop(0, nblocks // per, step, 0)
    first, block_at = start_ref[0], start_ref[1]
    row_parts = near_ref.shape[1]
    for s in range(supers):

        def around(r, carry, s=s):
            for k in range(2):
                near_ref[s, r, :, k * 128 : (k + 1) * 128] = placed_ref[s, r * (nblocks // row_parts) + block_at + k]
            return carry

        lax.fori_loop(0, row_parts, around, 0)
        for k in range(per):
            part_ref[s, :, k * 128 : (k + 1) * 128] = placed_ref[s, first + k]


def place(blocks, occupancy, row_block, starts, row_parts):
    devices, supers, per, width_part, tall = blocks.shape
    smem = pl.BlockSpec(memory_space=pltpu.SMEM)
    vmem = pl.BlockSpec(memory_space=pltpu.VMEM)
    return pl.pallas_call(
        place_kernel,
        out_shape=(
            jax.ShapeDtypeStruct((supers, row_parts, width_part, 2 * tall), blocks.dtype),
            jax.ShapeDtypeStruct((supers, width_part, per * tall), blocks.dtype),
        ),
        in_specs=[smem, smem, smem, vmem],
        out_specs=(vmem, vmem),
        scratch_shapes=[pltpu.VMEM((supers, devices * per, width_part, tall), blocks.dtype)],
        compiler_params=pltpu.CompilerParams(vmem_limit_bytes=GRANT),
        name="place",
    )(row_block, occupancy, starts, blocks)


def dot_high(a, b):
    return jnp.dot(a, b, precision=highest)


def per_device(inverse_block, factor_cols, occupancy, row_block, coupling, diag_inverse):
    column = lax.axis_index("col")
    row_parts = lax.axis_size("row")
    col_parts = lax.axis_size("col")
    local_rows = inverse_block.shape[0]
    rows_total = local_rows * row_parts
    supers, span, width_part = factor_cols.shape
    width = width_part * row_parts
    tile = local_rows // col_parts
    diag_cols = diag_inverse.shape[2]
    per = span // 128

    packed = jnp.transpose(factor_cols.reshape(supers, per, 128, width_part), (0, 1, 3, 2))
    block_at = jnp.minimum(column * tile // 128, local_rows // 128 - 2)
    starts = jnp.stack([column * per, block_at]).astype(jnp.int32)
    near, part = place(gather_col(packed), occupancy, row_block, starts, row_parts)
    outgoing = lax.dynamic_slice_in_dim(near, column * tile - block_at * 128, tile, 3)
    outgoing = jnp.transpose(outgoing, (1, 0, 2, 3)).reshape(ZS, YH, -1, 128)
    panel = gather_row(part).reshape(supers * width, span)
    term = lax.dot_general(
        inverse_block, panel, (((1,), (1,)), ((), ())), preferred_element_type=jnp.float32
    )
    summed, arrived = scatter_sum(term.reshape(col_parts, tile, supers * width), 2, outgoing)
    arrived = jnp.transpose(arrived.reshape(row_parts, supers, width_part, tile), (1, 0, 2, 3))
    own_rows = arrived.reshape(supers, width, tile).astype(jnp.float32)

    columns = []
    chain = []
    here = (jnp.arange(col_parts) == column) & (lax.axis_index("row") == 0)
    here = here.astype(jnp.float32)[:, None, None]
    for s in range(supers):
        product = summed[:, s * width : (s + 1) * width]
        own = own_rows[s]
        if s == 0:
            current = -product
            inner = dot_high(current.T, own.T)
        else:
            link = coupling[s - 1].astype(jnp.float32)
            coupled = dot_high(columns[-1], link)
            current = -(product + coupled)
            inner = dot_high(current.T, own.T) - dot_high(own, coupled)
        embedded = (here * diag_inverse[s].T[None]).reshape(width, width)
        total = embedded - inner / rows_total
        if s > 0:
            total = total + dot_high(link.T, dot_high(chain[-1], link))
        columns.append(current)
        chain.append(total)
    partial = jnp.stack([t.reshape(col_parts, diag_cols, width) for t in chain], axis=1)
    (mine,) = scatter_sum(partial.reshape(col_parts, supers * diag_cols, width), 4)
    diagonals = jnp.transpose(sum_row(mine, 6).reshape(supers, diag_cols, width), (0, 2, 1))
    return (jnp.stack(columns), diagonals)


def solution(mesh):
    in_specs = (P("row", "col"), P(None, "col", "row"), P(), P(), P(), P(None, None, "col"))
    out_specs = (P(None, ("row", "col"), None), P(None, None, "col"))
    return jax.shard_map(
        per_device, mesh=mesh, in_specs=in_specs, out_specs=out_specs, check_vma=False
    )
```

```python
import jax
import jax.numpy as jnp
from jax import lax
from jax.experimental import pallas as pl
from jax.experimental.pallas import tpu as pltpu
from jax.sharding import PartitionSpec as P

highest = lax.Precision.HIGHEST
MESH = pl.DeviceIdType.MESH
GRANT = 16 << 20
ZS, YH = 8, 4
CHIPS, XS = 8, 4


def greet(peers):
    barrier = pltpu.get_barrier_semaphore()
    for peer in peers:
        pl.semaphore_signal(barrier, inc=1, device_id=peer, device_id_type=MESH)
    pl.semaphore_wait(barrier, len(peers))


def push(src, dst, send_sem, recv_sem, device):
    return pltpu.make_async_remote_copy(
        src_ref=src,
        dst_ref=dst,
        send_sem=send_sem,
        recv_sem=recv_sem,
        device_id=device,
        device_id_type=MESH,
    )


def ring_position():
    row, col = lax.axis_index("row"), lax.axis_index("col")
    chip, core = col // 2, lax.rem(col, 2)
    x, y = lax.rem(chip, XS), chip // XS

    def at(dx, dy):
        return (y if dy == 0 else 1 - y) * XS + lax.rem(x + dx, XS)

    return row, core, at


NEAR = ((1, 0), (XS - 1, 0), (0, 1), (1, 1), (XS - 1, 1))


def gather_col_kernel(x_ref, out_ref, local_sem, send_sem, pass_sem, turn_sem, half_sem, recv_sem):
    row, core, at = ring_position()
    chip = at(0, 0)
    col = chip * 2 + core
    partner = (row, chip * 2 + 1 - core)
    half = x_ref.shape[0] // 2
    parts = (pl.ds(0, half), pl.ds(half, x_ref.shape[0] - half))
    greet([(row, at(*step) * 2 + core) for step in NEAR] + [partner])
    mine = pltpu.make_async_copy(x_ref, out_ref.at[col], local_sem)
    mine.start()
    copies = []

    def send(src, dst, sem, landing, device):
        copy = push(src, dst, sem, landing, device)
        copy.start()
        copies.append(copy)

    for j, step in enumerate(NEAR):
        send(x_ref, out_ref.at[col], send_sem.at[j], recv_sem.at[col], (row, at(*step) * 2 + core))
    send(x_ref, out_ref.at[col], pass_sem.at[0], recv_sem.at[col], partner)
    for j, step in enumerate(NEAR):
        slot = at(*step) * 2 + core
        push(x_ref, out_ref.at[slot], local_sem, recv_sem.at[slot], partner).wait_recv()
        if step[1] == 0:
            piece = out_ref.at[slot, parts[j]]
            for dy in range(2):
                device = (row, at(XS - step[0], dy) * 2 + core)
                send(piece, piece, turn_sem.at[j, dy], half_sem.at[j, dy], device)
        send(out_ref.at[slot], out_ref.at[slot], pass_sem.at[1 + j], recv_sem.at[slot], partner)
    for dy in range(2):
        slot = at(2, dy) * 2 + core
        for j in range(2):
            piece = out_ref.at[slot, parts[j]]
            push(piece, piece, local_sem, half_sem.at[j, dy], partner).wait_recv()
        send(out_ref.at[slot], out_ref.at[slot], pass_sem.at[6 + dy], recv_sem.at[slot], partner)
    for step in ((0, 0),) + NEAR + ((2, 0), (2, 1)):
        slot = at(*step) * 2 + 1 - core
        push(x_ref, out_ref.at[slot], local_sem, recv_sem.at[slot], partner).wait_recv()
    for copy in copies:
        copy.wait_send()
    mine.wait()


def gather_col(x):
    return pl.pallas_call(
        gather_col_kernel,
        out_shape=jax.ShapeDtypeStruct((CHIPS * 2,) + x.shape, x.dtype),
        in_specs=[pl.BlockSpec(memory_space=pl.ANY)],
        out_specs=pl.BlockSpec(memory_space=pl.ANY),
        scratch_shapes=[
            pltpu.SemaphoreType.DMA,
            pltpu.SemaphoreType.DMA((len(NEAR),)),
            pltpu.SemaphoreType.DMA((CHIPS,)),
            pltpu.SemaphoreType.DMA((2, 2)),
            pltpu.SemaphoreType.DMA((2, 2)),
            pltpu.SemaphoreType.DMA((CHIPS * 2,)),
        ],
        compiler_params=pltpu.CompilerParams(collective_id=0, has_side_effects=True, vmem_limit_bytes=GRANT),
        name="gather_col",
    )(x)


def gather_row_kernel(x_ref, out_ref, local_sem, send_sem, wide_sem, thin_sem):
    row, col = lax.axis_index("row"), lax.axis_index("col")
    z, y = row // YH, lax.rem(row, YH)
    last = x_ref.shape[0] - 1
    parts = (pl.ds(0, last), pl.ds(last, 1))
    sems = (wide_sem, thin_sem)

    def at(dz, dy):
        return lax.rem(z + dz + ZS, ZS) * YH + lax.rem(y + dy + YH, YH)

    def device(dz, dy):
        return (at(dz, dy), col)

    right, left, up, down = device(1, 0), device(-1, 0), device(0, 1), device(0, -1)
    greet([right, left, up, down])
    mine = pltpu.make_async_copy(x_ref, out_ref.at[:, row], local_sem)
    mine.start()
    copies = []

    def send(src, dst, landing, where):
        copy = push(src, dst, send_sem.at[len(copies)], landing, where)
        copy.start()
        copies.append(copy)

    def block(kind, slot):
        return out_ref.at[parts[kind], slot]

    def onward(kind, slot, where, first=False):
        src = x_ref.at[parts[kind]] if first else block(kind, slot)
        send(src, block(kind, slot), sems[kind].at[slot], where)

    def arrive(kind, slot):
        piece = block(kind, slot)
        push(piece, piece, local_sem, sems[kind].at[slot], right).wait_recv()

    for where in (right, left):
        onward(1, row, where, True)
    for where in (up, down):
        onward(0, row, where, True)
    for where in (right, left):
        onward(0, row, where, True)
    for where in (up, down):
        onward(1, row, where, True)

    for dy in (-1, 1, 2):
        slot = at(0, dy)
        arrive(0, slot)
        if dy == -1:
            onward(0, slot, up)
        onward(0, slot, right)
        onward(0, slot, left)

    half = ZS // 2

    def cross(dz):
        arrive(1, at(dz, -1))
        if dz % 2 == 0:
            onward(1, at(dz, -1), up)
        arrive(1, at(dz, 1))
        if dz % 2 == 1:
            onward(1, at(dz, 1), down)

    for hop in range(1, half + 1):
        for dz, far, where in ((-hop, half, right), (hop, ZS - 1 - half, left)):
            if hop <= far:
                slot = at(dz, 0)
                arrive(1, slot)
                if hop < far:
                    onward(1, slot, where)
                onward(1, slot, up)
                onward(1, slot, down)
        for j in range(YH):
            far_right = half - j % 2
            for dz, far, where in ((-hop, far_right, right), (hop, ZS - 1 - far_right, left)):
                if hop <= far:
                    arrive(0, at(dz, j))
                if hop < far:
                    onward(0, at(dz, j), where)
        cross(hop - 1)
        if hop > 1:
            cross(1 - hop)
    cross(half)
    for dz in range(1 - half, half + 1):
        arrive(1, at(dz, 2))
    for copy in copies:
        copy.wait_send()
    mine.wait()


def gather_row(x):
    supers, width_part, span = x.shape
    return pl.pallas_call(
        gather_row_kernel,
        out_shape=jax.ShapeDtypeStruct((supers, ZS * YH, width_part, span), x.dtype),
        in_specs=[pl.BlockSpec(memory_space=pl.ANY)],
        out_specs=pl.BlockSpec(memory_space=pl.ANY),
        scratch_shapes=[
            pltpu.SemaphoreType.DMA,
            pltpu.SemaphoreType.DMA((80,)),
            pltpu.SemaphoreType.DMA((ZS * YH,)),
            pltpu.SemaphoreType.DMA((ZS * YH,)),
        ],
        compiler_params=pltpu.CompilerParams(collective_id=1, has_side_effects=True, vmem_limit_bytes=GRANT),
        name="gather_row",
    )(x)


def swap_core_kernel(x_ref, out_ref, got, send_sem, recv_sem):
    row, col = lax.axis_index("row"), lax.axis_index("col")
    chip, core = col // 2, lax.rem(col, 2)
    partner = (row, chip * 2 + 1 - core)
    greet([partner])
    copy = push(x_ref.at[:, 1 - core], got, send_sem, recv_sem, partner)
    copy.start()
    copy.wait()

    def add(i, carry):
        rows = pl.ds(pl.multiple_of(i * 8, 8), 8)
        for j in range(CHIPS):
            out_ref[j, rows] = x_ref[j, core, rows] + got[j, rows]
        return carry

    lax.fori_loop(0, x_ref.shape[2] // 8, add, 0)


def swap_core(x, ident):
    shape = x.shape[:1] + x.shape[2:]
    return pl.pallas_call(
        swap_core_kernel,
        out_shape=jax.ShapeDtypeStruct(shape, x.dtype),
        in_specs=[pl.BlockSpec(memory_space=pltpu.VMEM)],
        out_specs=pl.BlockSpec(memory_space=pltpu.VMEM),
        scratch_shapes=[pltpu.VMEM(shape, x.dtype), pltpu.SemaphoreType.DMA, pltpu.SemaphoreType.DMA],
        compiler_params=pltpu.CompilerParams(collective_id=ident, has_side_effects=True, vmem_limit_bytes=GRANT),
        name="swap_core_%d" % ident,
    )(x)


class RowExchange:
    def __init__(self, rows_ref, own_ref, staged, local_sem, send_sem, z_sem, y_sem):
        self.rows, self.own, self.staged = rows_ref, own_ref, staged
        self.local_sem, self.send_sem, self.z_sem, self.y_sem = local_sem, send_sem, z_sem, y_sem
        row, self.col = lax.axis_index("row"), lax.axis_index("col")
        self.z, self.y = row // YH, lax.rem(row, YH)
        self.over_z = [lax.rem(self.z + j, ZS) for j in range(1, ZS)]
        self.over_y = [lax.rem(self.y + j, YH) for j in range(1, YH)]
        self.z_devices = [(other * YH + self.y, self.col) for other in self.over_z]
        self.y_devices = [(self.z * YH + other, self.col) for other in self.over_y]
        self.copies = []

    def send(self, *args):
        copy = push(*args)
        copy.start()
        self.copies.append(copy)

    def begin(self):
        self.mine = pltpu.make_async_copy(self.rows.at[self.z], self.staged.at[self.z], self.local_sem)
        self.mine.start()
        for j, other in enumerate(self.over_z):
            self.send(self.rows.at[other], self.staged.at[self.z], self.send_sem.at[j], self.z_sem.at[self.z], self.z_devices[j])

    def turn(self):
        self.mine.wait()
        for j, other in enumerate(self.over_z):
            push(self.rows.at[other], self.staged.at[other], self.local_sem, self.z_sem.at[other], self.z_devices[j]).wait_recv()
        self.mine = pltpu.make_async_copy(self.staged.at[:, self.y], self.own.at[:, self.y], self.local_sem)
        self.mine.start()
        for j, other in enumerate(self.over_y):
            self.send(self.staged.at[:, other], self.own.at[:, self.y], self.send_sem.at[ZS - 1 + j], self.y_sem.at[self.y], self.y_devices[j])

    def end(self):
        for j, other in enumerate(self.over_y):
            push(self.staged.at[:, other], self.own.at[:, other], self.local_sem, self.y_sem.at[other], self.y_devices[j]).wait_recv()
        for copy in self.copies:
            copy.wait_send()
        self.mine.wait()


def swap_chips_kernel(x_ref, sum_ref, out_ref, relay, local_sem, send_sem, away_sem, turn_sem, relay_sem, half_sem, recv_sem, ride=None):
    row, core, at = ring_position()
    chip = at(0, 0)
    rows = x_ref.shape[1]
    cut = rows // 16 * 8
    parts = (pl.ds(0, cut), pl.ds(cut, rows - cut))
    sizes = (cut, rows - cut)

    def device(step):
        return (row, at(*step) * 2 + core)

    greet([device(step) for step in NEAR] + (ride.z_devices + ride.y_devices if ride else []))
    if ride:
        ride.begin()
    copies = []

    def send(src, dst, sem, landing, device):
        copy = push(src, dst, sem, landing, device)
        copy.start()
        copies.append(copy)

    def held(j, dy):
        return relay.at[j, dy, pl.ds(0, sizes[j])]

    for dy in range(2):
        for j in range(2):
            send(x_ref.at[at(2, dy), parts[j]], held(j, dy), away_sem.at[j, dy], relay_sem.at[j, dy], device(NEAR[j]))
    for j, step in enumerate(NEAR):
        send(x_ref.at[at(*step)], out_ref.at[chip], send_sem.at[j], recv_sem.at[chip], device(step))
    for dy in range(2):
        for j in range(2):
            origin = at(XS - NEAR[j][0], 0)
            push(held(j, dy), held(j, dy), local_sem, relay_sem.at[j, dy], device(NEAR[j])).wait_recv()
            target = device((NEAR[j][0], dy))
            send(held(j, dy), out_ref.at[origin, parts[j]], turn_sem.at[j, dy], half_sem.at[j, dy], target)
    if ride:
        ride.turn()
    for step in NEAR:
        other = at(*step)
        push(x_ref.at[other], out_ref.at[other], local_sem, recv_sem.at[other], device(step)).wait_recv()
    for dy in range(2):
        for j in range(2):
            piece = out_ref.at[at(2, dy), parts[j]]
            push(piece, piece, local_sem, half_sem.at[j, dy], device(NEAR[0])).wait_recv()
    others = [at(*step) for step in NEAR + ((2, 0), (2, 1))]

    def add(i, carry):
        span = pl.ds(pl.multiple_of(i * 8, 8), 8)
        total = x_ref[chip, span]
        for other in others:
            total = total + out_ref[other, span]
        sum_ref[span] = total
        return carry

    lax.fori_loop(0, rows // 8, add, 0)
    for copy in copies:
        copy.wait_send()
    if ride:
        ride.end()


def swap_chips(x, ident, rows=None):
    chips, tall, lanes = x.shape
    dma = pltpu.SemaphoreType.DMA
    shapes = [jax.ShapeDtypeStruct(x.shape[1:], x.dtype)]
    scratch = [
        pltpu.VMEM(x.shape, x.dtype),
        pltpu.VMEM((2, 2, tall - tall // 16 * 8, lanes), x.dtype),
        dma,
        dma((len(NEAR),)),
        dma((2, 2)),
        dma((2, 2)),
        dma((2, 2)),
        dma((2, 2)),
        dma((chips,)),
    ]
    own = len(scratch)
    operands = [x]
    if rows is not None:
        operands.append(rows)
        shapes.append(jax.ShapeDtypeStruct(rows.shape, rows.dtype))
        scratch += [pltpu.VMEM(rows.shape, rows.dtype), dma, dma((ZS + YH - 2,)), dma((ZS,)), dma((YH,))]

    def kernel(*refs):
        count = len(operands)
        arrays, rest = refs[: 2 * count], refs[2 * count :]
        ride = RowExchange(arrays[1], arrays[3], *rest[own:]) if count == 2 else None
        swap_chips_kernel(arrays[0], arrays[count], *rest[:own], ride=ride)

    vmem = pl.BlockSpec(memory_space=pltpu.VMEM)
    return pl.pallas_call(
        kernel,
        out_shape=shapes,
        in_specs=[vmem] * len(operands),
        out_specs=[vmem] * len(operands),
        scratch_shapes=scratch,
        compiler_params=pltpu.CompilerParams(collective_id=ident, has_side_effects=True, vmem_limit_bytes=GRANT),
        name="swap_chips_%d" % ident,
    )(*operands)


def sum_row_kernel(x_ref, out_ref, got_y, mid, got_z, whole, y_send, y_recv, z_send, z_recv, send_sem, recv_sem):
    row, col = lax.axis_index("row"), lax.axis_index("col")
    z, y = row // YH, lax.rem(row, YH)
    zs = [lax.rem(z + j, ZS) for j in range(1, ZS)]
    ys = [lax.rem(y + j, YH) for j in range(1, YH)]
    tall = [(other * YH + y, col) for other in zs]
    flat = [(z * YH + other, col) for other in ys]
    greet(tall + flat)
    copies = []

    def send(*args):
        copy = push(*args)
        copy.start()
        copies.append(copy)

    for j, other in enumerate(zs):
        send(x_ref.at[other], got_z.at[z], z_send.at[j], z_recv.at[z], tall[j])
    for j, other in enumerate(zs):
        push(x_ref.at[other], got_z.at[other], z_send.at[j], z_recv.at[other], tall[j]).wait_recv()
    total = x_ref[z]
    for other in zs:
        total = total + got_z[other]
    mid[...] = total
    for j, other in enumerate(ys):
        send(mid.at[other], got_y.at[y], y_send.at[j], y_recv.at[y], flat[j])
    for j, other in enumerate(ys):
        push(mid.at[other], got_y.at[other], y_send.at[j], y_recv.at[other], flat[j]).wait_recv()
    total = mid[y]
    for other in ys:
        total = total + got_y[other]
    whole[...] = total
    out_ref[z, y] = total
    first = len(copies)

    def spread(src, at, where):
        send(src, out_ref.at[at], send_sem.at[len(copies) - first], recv_sem.at[at], where)

    for where in flat + tall:
        spread(whole, (z, y), where)
    for lane in ys:
        push(whole, out_ref.at[z, lane], y_send.at[0], recv_sem.at[z, lane], flat[0]).wait_recv()
        for where in tall:
            spread(out_ref.at[z, lane], (z, lane), where)
    for there in zs:
        for lane in [y] + ys:
            push(whole, out_ref.at[there, lane], y_send.at[0], recv_sem.at[there, lane], flat[0]).wait_recv()
    for copy in copies:
        copy.wait_send()


def sum_row(x, ident):
    rows, lanes = x.shape
    grid = x.reshape(ZS, YH, rows // (YH * ZS), lanes)
    dma = pltpu.SemaphoreType.DMA
    vmem = pl.BlockSpec(memory_space=pltpu.VMEM)
    whole = pl.pallas_call(
        sum_row_kernel,
        out_shape=jax.ShapeDtypeStruct((ZS, YH) + grid.shape[2:], x.dtype),
        in_specs=[vmem],
        out_specs=vmem,
        scratch_shapes=[
            pltpu.VMEM(grid.shape[1:], x.dtype),
            pltpu.VMEM(grid.shape[1:], x.dtype),
            pltpu.VMEM(grid.shape, x.dtype),
            pltpu.VMEM(grid.shape[2:], x.dtype),
            dma((YH - 1,)),
            dma((YH,)),
            dma((ZS - 1,)),
            dma((ZS,)),
            dma((ZS * YH - 1,)),
            dma((ZS, YH)),
        ],
        compiler_params=pltpu.CompilerParams(collective_id=ident, has_side_effects=True, vmem_limit_bytes=GRANT),
        name="sum_row",
    )(grid)
    return whole.reshape(rows, lanes)


def scatter_sum(x, ident, rows=None):
    return swap_chips(swap_core(x.reshape((CHIPS, 2) + x.shape[1:]), ident), ident + 1, rows)


def place_kernel(row_block_ref, occupancy_ref, start_ref, blocks_ref, near_ref, part_ref, placed_ref):
    supers, nblocks = placed_ref.shape[:2]
    per = blocks_ref.shape[2]
    for s in range(supers):

        def step(device, carry, s=s):
            for k in range(per):
                b = device * per + k
                block = blocks_ref[device, s, k]
                keep = occupancy_ref[s, b] > 0
                placed_ref[s, row_block_ref[s, b]] = jnp.where(keep, block, jnp.zeros_like(block))
            return carry

        lax.fori_loop(0, nblocks // per, step, 0)
    first, block_at = start_ref[0], start_ref[1]
    row_parts = near_ref.shape[1]
    for s in range(supers):

        def around(r, carry, s=s):
            for k in range(2):
                near_ref[s, r, :, k * 128 : (k + 1) * 128] = placed_ref[s, r * (nblocks // row_parts) + block_at + k]
            return carry

        lax.fori_loop(0, row_parts, around, 0)
        for k in range(per):
            part_ref[s, :, k * 128 : (k + 1) * 128] = placed_ref[s, first + k]


def place(blocks, occupancy, row_block, starts, row_parts):
    devices, supers, per, width_part, tall = blocks.shape
    smem = pl.BlockSpec(memory_space=pltpu.SMEM)
    vmem = pl.BlockSpec(memory_space=pltpu.VMEM)
    return pl.pallas_call(
        place_kernel,
        out_shape=(
            jax.ShapeDtypeStruct((supers, row_parts, width_part, 2 * tall), blocks.dtype),
            jax.ShapeDtypeStruct((supers, width_part, per * tall), blocks.dtype),
        ),
        in_specs=[smem, smem, smem, vmem],
        out_specs=(vmem, vmem),
        scratch_shapes=[pltpu.VMEM((supers, devices * per, width_part, tall), blocks.dtype)],
        compiler_params=pltpu.CompilerParams(vmem_limit_bytes=GRANT),
        name="place",
    )(row_block, occupancy, starts, blocks)


def dot_high(a, b):
    return jnp.dot(a, b, precision=highest)


def per_device(inverse_block, factor_cols, occupancy, row_block, coupling, diag_inverse):
    column = lax.axis_index("col")
    row_parts = lax.axis_size("row")
    col_parts = lax.axis_size("col")
    local_rows = inverse_block.shape[0]
    rows_total = local_rows * row_parts
    supers, span, width_part = factor_cols.shape
    width = width_part * row_parts
    tile = local_rows // col_parts
    diag_cols = diag_inverse.shape[2]
    per = span // 128

    packed = jnp.transpose(factor_cols.reshape(supers, per, 128, width_part), (0, 1, 3, 2))
    block_at = jnp.minimum(column * tile // 128, local_rows // 128 - 2)
    starts = jnp.stack([column * per, block_at]).astype(jnp.int32)
    near, part = place(gather_col(packed), occupancy, row_block, starts, row_parts)
    outgoing = lax.dynamic_slice_in_dim(near, column * tile - block_at * 128, tile, 3)
    outgoing = jnp.transpose(outgoing, (1, 0, 2, 3)).reshape(ZS, YH, -1, 128)
    panel = gather_row(part).reshape(supers * width, span)
    term = lax.dot_general(
        inverse_block, panel, (((1,), (1,)), ((), ())), preferred_element_type=jnp.float32
    )
    summed, arrived = scatter_sum(term.reshape(col_parts, tile, supers * width), 2, outgoing)
    arrived = jnp.transpose(arrived.reshape(row_parts, supers, width_part, tile), (1, 0, 2, 3))
    own_rows = arrived.reshape(supers, width, tile).astype(jnp.float32)

    columns = []
    chain = []
    here = (jnp.arange(col_parts) == column) & (lax.axis_index("row") == 0)
    here = here.astype(jnp.float32)[:, None, None]
    for s in range(supers):
        product = summed[:, s * width : (s + 1) * width]
        own = own_rows[s]
        if s == 0:
            current = -product
            inner = dot_high(current.T, own.T)
        else:
            link = coupling[s - 1].astype(jnp.float32)
            coupled = dot_high(columns[-1], link)
            current = -(product + coupled)
            inner = dot_high(current.T, own.T) - dot_high(own, coupled)
        embedded = (here * diag_inverse[s].T[None]).reshape(width, width)
        total = embedded - inner / rows_total
        if s > 0:
            total = total + dot_high(link.T, dot_high(chain[-1], link))
        columns.append(current)
        chain.append(total)
    partial = jnp.stack([t.reshape(col_parts, diag_cols, width) for t in chain], axis=1)
    (mine,) = scatter_sum(partial.reshape(col_parts, supers * diag_cols, width), 4)
    diagonals = jnp.transpose(sum_row(mine, 6).reshape(supers, diag_cols, width), (0, 2, 1))
    return (jnp.stack(columns), diagonals)


def solution(mesh):
    in_specs = (P("row", "col"), P(None, "col", "row"), P(), P(), P(), P(None, None, "col"))
    out_specs = (P(None, ("row", "col"), None), P(None, None, "col"))
    return jax.shard_map(
        per_device, mesh=mesh, in_specs=in_specs, out_specs=out_specs, check_vma=False
    )
```
